512 devices in a mesh: leaf: 8 (over y), row: 8 (over z), col: 8 (over x, core).
Axes of the slice: x: 4, y: 8, z: 8, core: 2. Of those that a mesh axis runs over, the one named last changes fastest.
Arguments:
- child_front: float32 [8, 4096, 4096], P('leaf', 'row', 'col'), may hold values from -2 to 4, as said below
- parent_front: float32 [8192, 1, 64, 128], P('row', None, ('leaf', 'col')), may hold values from -2 to 4, as said below
- block_map: int32 [8, 30], replicated, may hold values from 0 to 63, as said below
Outputs:
- child_factor: float32 [8, 4096, 256], P('leaf', 'row')
- parent_out: float32 [8192, 1, 64, 128], P('row', None, ('leaf', 'col'))
The draws below stay inside these ranges and needn't reach their ends.
Inputs may be any that keep to these rules, and one draw needn't show every extreme that they name: `child_front`: each child front is symmetric positive definite, with smallest eigenvalue above 0.1. `parent_front`: viewed as a 8192 x 8192 matrix, the parent front is symmetric positive definite, with smallest eigenvalue above 0.1. `block_map`: row c lists, in order, the parent block that receives each of the 30 trailing blocks of child front c; the entries of a row are distinct parent blocks. Put 2 empty blocks in front of a row and cut it into aligned groups of 4: in every group at most 1 entries share the value of entry // 8, and at most 1 share the value of entry modulo 8; both bounds are reached.
All inputs are finite; a program needn't handle non-finite values.
Results may differ from the reference program's by a relative error of at most 0.0001.
Values sent between devices are 32-bit elements; how exact they have to be, the bound alone decides.
No kernel may reach another device: no remote copies, remote signals or barrier semaphores. Data moves between devices by JAX's collectives and lax.ppermute only.
A program may use at most 64 MiB of HBM per device.

```python
import jax
import jax.numpy as jnp
from jax import lax

FC = 4096
FP = 8192
PANEL = 256
BLOCK = 128
CHILDREN = 8
GRID = 8
NB_C = 32
MB = 30
CB = 4
PR = 8
NCD = 64
KB = 1
SPREAD = 1


def symmetric_front(key, order):
    inner_width = max(order // 8, 64)
    factor_key, lift_key, noise_key = jax.random.split(key, 3)
    factor = jax.random.normal(factor_key, (order, inner_width), jnp.float32)
    diagonal = jax.random.uniform(lift_key, (order,), jnp.float32, 0.25, 0.65)
    noise = jax.random.normal(noise_key, (order, order), jnp.float32)
    coupled = jnp.dot(factor, factor.T, precision=lax.Precision.HIGHEST, preferred_element_type=jnp.float32) / inner_width
    coupled = 0.5 * (coupled + coupled.T)
    rough_part = (noise + noise.T) * (0.03 / jnp.sqrt(2.0 * order))
    return coupled + rough_part + jnp.diag(diagonal)


def draw_child_front(key, part):
    base = jax.random.fold_in(key, 11)
    fronts = [symmetric_front(jax.random.fold_in(base, child), FC) for child in range(CHILDREN)]
    return jnp.stack(fronts)


def draw_parent_front(key, part):
    whole_front = symmetric_front(jax.random.fold_in(key, 101), FP)
    return whole_front.reshape(FP, KB, NCD, BLOCK)


def draw_block_map(key, part):
    base = jax.random.fold_in(key, 202)
    listing = []
    for child in range(CHILDREN):
        child_key = jax.random.fold_in(base, child)
        key_row, key_col, key_extra, key_slot = jax.random.split(child_key, 4)
        perm_row = jax.random.permutation(key_row, GRID)
        perm_col = jax.random.permutation(key_col, GRID)
        perm_extra = jax.random.permutation(key_extra, SPREAD)
        slot_keys = jax.random.split(key_slot, GRID)
        slot_perm = jax.vmap(lambda one_key: jax.random.permutation(one_key, CB))(slot_keys)
        position = jnp.arange(NB_C, dtype=jnp.int32)
        group = position // CB
        slot = slot_perm[group, position % CB]
        first = (group + slot) % GRID
        second = (2 * group + slot) % GRID
        extra = slot // GRID
        target = perm_row[first] * PR + perm_extra[extra] * GRID + perm_col[second]
        listing.append(target[NB_C - MB:])
    return jnp.stack(listing).astype(jnp.int32)


def setup_inputs(seed: int = 0) -> dict:
    keys = jax.random.split(jax.random.key(seed), 4)
    return {
        "child_front": draw_child_front(jax.random.fold_in(keys[3], 71), 0),
        "parent_front": draw_parent_front(jax.random.fold_in(keys[3], 71), 0),
        "block_map": draw_block_map(jax.random.fold_in(keys[3], 71), 0),
    }


def matmul(left, right):
    return jnp.dot(left.astype(jnp.float32), right.astype(jnp.float32), precision=lax.Precision.HIGHEST, preferred_element_type=jnp.float32)

def factor_panel(front):
    lower_factor = jnp.linalg.cholesky(front[:PANEL, :PANEL])
    identity = jnp.eye(PANEL, dtype=jnp.float32)
    inverse = jax.scipy.linalg.solve_triangular(lower_factor, identity, lower=True)
    panel = matmul(front[:, :PANEL], inverse.T)
    upper = matmul(inverse, front[:PANEL, PANEL:])
    schur = front[PANEL:, PANEL:] - matmul(panel[PANEL:], upper)
    return (panel, schur)

def reference(child_front, parent_front, block_map):
    assembled = parent_front.reshape(FP, FP)
    offsets = jnp.arange(BLOCK, dtype=jnp.int32)
    factors = []
    for child in range(CHILDREN):
        panel, contribution = factor_panel(child_front[child])
        factors.append(panel)
        targets = (block_map[child].astype(jnp.int32)[:, None] * BLOCK + offsets[None, :]).reshape(-1)
        assembled = assembled.at[targets[:, None], targets[None, :]].add(contribution)
    panel, schur = factor_panel(assembled)
    result = assembled.at[PANEL:, PANEL:].set(schur).at[:, :PANEL].set(panel)
    return (jnp.stack(factors), result.reshape(FP, KB, NCD, BLOCK))
```

```python
import jax
import jax.numpy as jnp
from jax import lax
from jax.experimental import pallas as pl
from jax.experimental.pallas import tpu as pltpu
from jax.sharding import Mesh
from jax.sharding import PartitionSpec as P

FP = 8192
PANEL = 256
BLOCK = 128
COL = ("col_0", "col_1")
ROW_COL = ("row", "col_0", "col_1")
LEAF_COL = ("leaf", "col_0", "col_1")
LEAF_ROW = ("leaf", "row")
HIGHEST = lax.Precision.HIGHEST
STEP = 64
GROUP = 8


def matmul(left, right):
    return jnp.dot(left, right, precision=HIGHEST, preferred_element_type=jnp.float32)


def matmul_nt(left, right):
    return lax.dot_general(
        left,
        right,
        (((1,), (1,)), ((), ())),
        precision=HIGHEST,
        preferred_element_type=jnp.float32,
    )


def matmul_tn(left, right):
    return lax.dot_general(
        left,
        right,
        (((0,), (0,)), ((), ())),
        precision=HIGHEST,
        preferred_element_type=jnp.float32,
    )


def exchange(value, axes):
    return lax.all_to_all(value, axes, split_axis=0, concat_axis=0, tiled=True)


def spread(value, axes, count):
    return exchange(jnp.broadcast_to(value[None], (count, *value.shape)), axes)


def eliminate(tile, eye, step):
    width = 2 * step
    row = lax.broadcasted_iota(jnp.int32, (step, width), 0)
    work = jnp.concatenate([tile, eye], axis=1)
    pivots = jnp.ones((step, width), jnp.float32)

    def tall(value):
        return jnp.concatenate([value] * (step // 8), axis=0)

    for first in range(0, step, GROUP):
        span = range(GROUP)
        cols = [
            jnp.broadcast_to(work[:, first + i : first + i + 1], (step, width)) for i in span
        ]
        rows = [jnp.broadcast_to(work[first + i : first + i + 1, :], (8, width)) for i in span]
        small = {}
        for i in span:
            for j in range(i, GROUP):
                small[i, j] = jnp.broadcast_to(cols[i][first + j : first + j + 1, :], (8, width))
        ratio = {}
        recip = []
        for i in span:
            recip.append(1.0 / small[i, i])
            for j in range(i + 1, GROUP):
                ratio[i, j] = small[i, j] * recip[i]
            for j in range(i + 1, GROUP):
                for k in range(j, GROUP):
                    small[j, k] = small[j, k] - ratio[i, j] * small[i, k]
        update = None
        for i in span:
            scaled = jnp.where(row > first + i, cols[i] * tall(recip[i]), 0.0)
            pivots = jnp.where(row == first + i, tall(small[i, i]), pivots)
            for j in range(i + 1, GROUP):
                cols[j] = cols[j] - cols[i] * tall(ratio[i, j])
                rows[j] = rows[j] - ratio[i, j] * rows[i]
            term = scaled * tall(rows[i])
            update = term if update is None else update + term
        work = work - update
    return work[:, step:width] * lax.rsqrt(pivots)[:, :step]


def inverse_kernel(corner_ref, out_ref, work_ref):
    size = corner_ref.shape[0]
    step = STEP
    row = lax.broadcasted_iota(jnp.int32, (size, size), 0)
    col = lax.broadcasted_iota(jnp.int32, (size, size), 1)
    work_ref[:, :size] = corner_ref[...]
    work_ref[:, size:] = (row == col).astype(jnp.float32)
    small_row = lax.broadcasted_iota(jnp.int32, (step, step), 0)
    small_col = lax.broadcasted_iota(jnp.int32, (step, step), 1)
    eye = (small_row == small_col).astype(jnp.float32)
    for start in range(0, size, step):
        stop = start + step
        lead = eliminate(work_ref[start:stop, start:stop], eye, step)
        upper = matmul(lead, work_ref[start:stop, :])
        out_ref[start:stop, :] = upper[:, size:]
        if stop < size:
            work_ref[stop:, :] = work_ref[stop:, :] - matmul_tn(upper[:, stop:size], upper)


def lower_inverse(corner):
    size = corner.shape[0]
    return pl.pallas_call(
        inverse_kernel,
        out_shape=jax.ShapeDtypeStruct((size, size), jnp.float32),
        scratch_shapes=[pltpu.VMEM((size, 2 * size), jnp.float32)],
        name="lower_inverse",
    )(corner)


def pick_kernel(index_ref, valid_ref, front_ref, out_ref):
    keep = valid_ref[pl.program_id(0)] > 0
    out_ref[0] = jnp.where(keep, front_ref[...], 0.0)


def pick_columns(index, valid, front):
    rows = front.shape[0]
    count = index.shape[0]
    return pl.pallas_call(
        pick_kernel,
        out_shape=jax.ShapeDtypeStruct((count, rows, BLOCK), jnp.float32),
        grid_spec=pltpu.PrefetchScalarGridSpec(
            num_scalar_prefetch=2,
            grid=(count,),
            in_specs=[pl.BlockSpec((rows, BLOCK), lambda i, index, valid: (0, index[i]))],
            out_specs=pl.BlockSpec((1, rows, BLOCK), lambda i, index, valid: (i, 0, 0)),
        ),
        name="pick_columns",
    )(index, valid, front)


def schur_kernel(
    slot_ref, slot_valid_ref, piece_ref, piece_valid_ref, cols_ref, factor_ref, block_ref, out_ref, tmp
):
    target = pl.program_id(0)
    live = slot_valid_ref[target] > 0

    @pl.when(live)
    def _():
        tmp[...] = cols_ref[0] - matmul_nt(factor_ref[...], block_ref[0])
        for dest in range(out_ref.shape[0]):
            start = pl.multiple_of(piece_ref[dest] * BLOCK, BLOCK)
            piece = tmp[pl.ds(start, BLOCK), :]
            out_ref[dest] = jnp.where(piece_valid_ref[dest] > 0, piece, 0.0)

    @pl.when(jnp.logical_not(live))
    def _():
        out_ref[...] = jnp.zeros_like(out_ref)


def schur_pieces(slot, slot_valid, piece, piece_valid, cols, factor, blocks):
    leaves = slot.shape[0]
    bands = piece.shape[0]
    rows = factor.shape[0]
    panel = factor.shape[1]
    return pl.pallas_call(
        schur_kernel,
        out_shape=jax.ShapeDtypeStruct((leaves * bands, BLOCK, BLOCK), jnp.float32),
        grid_spec=pltpu.PrefetchScalarGridSpec(
            num_scalar_prefetch=4,
            grid=(leaves,),
            in_specs=[
                pl.BlockSpec((1, rows, BLOCK), lambda i, s, sv, p, pv: (s[i], 0, 0)),
                pl.BlockSpec((rows, panel), lambda i, s, sv, p, pv: (0, 0)),
                pl.BlockSpec((1, BLOCK, panel), lambda i, s, sv, p, pv: (s[i], 0, 0)),
            ],
            out_specs=pl.BlockSpec((bands, BLOCK, BLOCK), lambda i, s, sv, p, pv: (i, 0, 0)),
            scratch_shapes=[pltpu.VMEM((rows, BLOCK), jnp.float32)],
        ),
        name="schur_pieces",
    )(slot, slot_valid, piece, piece_valid, cols, factor, blocks)


def place_kernel(slot_ref, parent_ref, blocks_ref, out_ref):
    step = pl.program_id(0)

    @pl.when(step == 0)
    def _():
        out_ref[...] = parent_ref[...]

    count = blocks_ref.shape[0]
    for item in range(count):
        slot = slot_ref[step * count + item]

        @pl.when(slot >= 0)
        def _(item=item, slot=slot):
            start = pl.multiple_of(slot * BLOCK, BLOCK)
            out_ref[pl.ds(start, BLOCK), :] += blocks_ref[item]


def place_blocks(slots, parent, blocks):
    total = blocks.shape[0]
    batch = 8
    rows = parent.shape[0]
    return pl.pallas_call(
        place_kernel,
        out_shape=jax.ShapeDtypeStruct(parent.shape, jnp.float32),
        grid_spec=pltpu.PrefetchScalarGridSpec(
            num_scalar_prefetch=1,
            grid=(total // batch,),
            in_specs=[
                pl.BlockSpec((rows, BLOCK), lambda i, slots: (0, 0)),
                pl.BlockSpec((batch, BLOCK, BLOCK), lambda i, slots: (i, 0, 0)),
            ],
            out_specs=pl.BlockSpec((rows, BLOCK), lambda i, slots: (0, 0)),
        ),
        name="place_blocks",
    )(slots, parent, blocks)


def locate(values, usable, count):
    hit = (values[..., None, :] == jnp.arange(count)[:, None]) & usable[..., None, :]
    index = jnp.sum(jnp.where(hit, jnp.arange(values.shape[-1]), 0), axis=-1)
    return index.astype(jnp.int32), jnp.any(hit, axis=-1)


def at(value, index, axis=0):
    return lax.dynamic_index_in_dim(value, index, axis, keepdims=False)


def per_device(child_front, parent_front, block_map):
    front = child_front[0]
    parent = parent_front[:, 0, 0, :]
    grid_rows = lax.axis_size("row")
    grid_cols = lax.axis_size(COL)
    leaves = lax.axis_size("leaf")
    row_id = lax.axis_index("row")
    col_id = lax.axis_index(COL)
    leaf_id = lax.axis_index("leaf")
    rows = front.shape[0]
    child_blocks = rows // BLOCK
    lead = PANEL // BLOCK
    plane = grid_rows * grid_cols
    parent_rows = parent.shape[0]

    padded = jnp.concatenate([jnp.full((leaves, lead), -1, jnp.int32), block_map], axis=1)
    maps = padded.reshape(leaves, grid_rows, child_blocks)
    usable = maps >= 0
    band = maps // grid_cols
    residue = maps % grid_cols
    lo_index, lo_valid = locate(residue, usable, grid_cols)
    hi_index, hi_valid = locate(band, usable, grid_rows)

    own_lo_index, own_lo_valid = at(lo_index, leaf_id), at(lo_valid, leaf_id)
    send_index, send_valid = at(own_lo_index, col_id), at(own_lo_valid, col_id)
    cols = exchange(
        pick_columns(send_index, send_valid.astype(jnp.int32), front), COL
    )

    corner = jnp.concatenate([front[:PANEL, :BLOCK], front[:PANEL, BLOCK:PANEL]], axis=0)
    corner = exchange(corner.reshape(plane, -1, BLOCK), ROW_COL)[0]
    corner = spread(corner, ROW_COL, plane).reshape(lead, PANEL, BLOCK)
    corner = jnp.concatenate([corner[i] for i in range(lead)], axis=1)
    inverse = lower_inverse(corner)
    piece = exchange(front[:, :PANEL].reshape(grid_cols, -1, PANEL), COL)[0]
    factor = spread(matmul_nt(piece, inverse), COL, grid_cols).reshape(rows, PANEL)

    column_index = at(own_lo_index, col_id, 1)
    column_valid = at(own_lo_valid, col_id, 1)
    mine = lax.dynamic_slice_in_dim(factor, at(column_index, row_id) * BLOCK, BLOCK, 0)
    blocks = spread(mine, "row", grid_rows)
    column_band = jnp.sum(
        jnp.where(
            jnp.arange(child_blocks) == column_index[:, None],
            at(band, leaf_id),
            0,
        ),
        axis=-1,
    )
    slot, slot_valid = locate(column_band, column_valid, leaves)
    pieces = schur_pieces(
        slot,
        slot_valid.astype(jnp.int32),
        at(at(hi_index, leaf_id), row_id),
        at(at(hi_valid, leaf_id), row_id).astype(jnp.int32),
        cols,
        factor,
        blocks,
    )
    arrived = exchange(pieces, LEAF_ROW)

    own_column = leaf_id * grid_cols + col_id
    present = jnp.any((maps == own_column) & usable, axis=(1, 2))
    row_index = at(hi_index, row_id, 2)
    row_valid = at(hi_valid, row_id, 2)
    row_slot = jnp.sum(
        jnp.where(jnp.arange(child_blocks) == row_index[..., None], residue, 0), axis=-1
    )
    slots = jnp.where(row_valid & present[:, None], row_slot, -1).astype(jnp.int32).reshape(-1)
    assembled = place_blocks(slots, parent, arrived)

    top = exchange(assembled[:PANEL].reshape(grid_rows, -1, BLOCK), "row")[0]
    top = spread(top, "row", grid_rows).reshape(PANEL, BLOCK)
    both = jnp.concatenate([assembled, top], axis=0)
    both = exchange(both.reshape(leaves * grid_cols, -1, BLOCK), LEAF_COL)[:lead]
    both = spread(both, LEAF_COL, leaves * grid_cols)
    both = jnp.concatenate(
        [both[:, i].reshape(parent_rows + PANEL, BLOCK) for i in range(lead)], axis=1
    )
    panel = both[:parent_rows]
    inverse_parent = lower_inverse(both[parent_rows:])
    parent_factor = matmul_nt(panel, inverse_parent)
    upper = matmul(inverse_parent, top)
    updated = assembled - matmul(parent_factor, upper)
    global_row = row_id * parent_rows + jnp.arange(parent_rows)
    kept = jnp.where((global_row < PANEL)[:, None], assembled, updated)
    result = kept
    for i in range(lead):
        result = jnp.where(
            own_column == i, parent_factor[:, i * BLOCK : (i + 1) * BLOCK], result
        )
    return (factor[None], result[:, None, None, :])


def solution(mesh):
    torus = Mesh(
        mesh.devices.reshape(mesh.shape["leaf"], mesh.shape["row"], 4, 2),
        ("leaf", "row", "col_0", "col_1"),
    )
    in_specs = (P("leaf", "row", COL), P("row", None, LEAF_COL, None), P())
    out_specs = (P("leaf", "row", None), P("row", None, LEAF_COL, None))
    return jax.shard_map(
        per_device, mesh=torus, in_specs=in_specs, out_specs=out_specs, check_vma=False
    )
```

```python
import jax
import jax.numpy as jnp
from jax import lax
from jax.experimental import pallas as pl
from jax.experimental.pallas import tpu as pltpu
from jax.sharding import Mesh
from jax.sharding import PartitionSpec as P

FP = 8192
PANEL = 256
BLOCK = 128
COL = ("col_0", "col_1")
LEAF_COL = ("leaf", "col_0", "col_1")
LEAF_ROW = ("leaf", "row")
HIGHEST = lax.Precision.HIGHEST
STEP = 64
GROUP = 8


def matmul(left, right):
    return jnp.dot(left, right, precision=HIGHEST, preferred_element_type=jnp.float32)


def matmul_nt(left, right):
    return lax.dot_general(
        left,
        right,
        (((1,), (1,)), ((), ())),
        precision=HIGHEST,
        preferred_element_type=jnp.float32,
    )


def matmul_tn(left, right):
    return lax.dot_general(
        left,
        right,
        (((0,), (0,)), ((), ())),
        precision=HIGHEST,
        preferred_element_type=jnp.float32,
    )


def exchange(value, axes):
    return lax.all_to_all(value, axes, split_axis=0, concat_axis=0, tiled=True)


def spread(value, axes, count):
    return exchange(jnp.broadcast_to(value[None], (count, *value.shape)), axes)


def eliminate(tile, eye, step):
    width = 2 * step
    row = lax.broadcasted_iota(jnp.int32, (step, width), 0)
    work = jnp.concatenate([tile, eye], axis=1)
    pivots = jnp.ones((step, width), jnp.float32)

    def tall(value):
        return jnp.concatenate([value] * (step // 8), axis=0)

    for first in range(0, step, GROUP):
        span = range(GROUP)
        cols = [
            jnp.broadcast_to(work[:, first + i : first + i + 1], (step, width)) for i in span
        ]
        rows = [jnp.broadcast_to(work[first + i : first + i + 1, :], (8, width)) for i in span]
        small = {}
        for i in span:
            for j in range(i, GROUP):
                small[i, j] = jnp.broadcast_to(cols[i][first + j : first + j + 1, :], (8, width))
        ratio = {}
        recip = []
        for i in span:
            recip.append(1.0 / small[i, i])
            for j in range(i + 1, GROUP):
                ratio[i, j] = small[i, j] * recip[i]
            for j in range(i + 1, GROUP):
                for k in range(j, GROUP):
                    small[j, k] = small[j, k] - ratio[i, j] * small[i, k]
        update = None
        for i in span:
            scaled = jnp.where(row > first + i, cols[i] * tall(recip[i]), 0.0)
            pivots = jnp.where(row == first + i, tall(small[i, i]), pivots)
            for j in range(i + 1, GROUP):
                cols[j] = cols[j] - cols[i] * tall(ratio[i, j])
                rows[j] = rows[j] - ratio[i, j] * rows[i]
            term = scaled * tall(rows[i])
            update = term if update is None else update + term
        work = work - update
    return work[:, step:width] * lax.rsqrt(pivots)[:, :step]


def inverse_kernel(corner_ref, out_ref, work_ref):
    size = corner_ref.shape[0]
    step = STEP
    row = lax.broadcasted_iota(jnp.int32, (size, size), 0)
    col = lax.broadcasted_iota(jnp.int32, (size, size), 1)
    work_ref[:, :size] = corner_ref[...]
    work_ref[:, size:] = (row == col).astype(jnp.float32)
    small_row = lax.broadcasted_iota(jnp.int32, (step, step), 0)
    small_col = lax.broadcasted_iota(jnp.int32, (step, step), 1)
    eye = (small_row == small_col).astype(jnp.float32)
    for start in range(0, size, step):
        stop = start + step
        lead = eliminate(work_ref[start:stop, start:stop], eye, step)
        upper = matmul(lead, work_ref[start:stop, :])
        out_ref[start:stop, :] = upper[:, size:]
        if stop < size:
            work_ref[stop:, :] = work_ref[stop:, :] - matmul_tn(upper[:, stop:size], upper)


def lower_inverse(corner):
    size = corner.shape[0]
    return pl.pallas_call(
        inverse_kernel,
        out_shape=jax.ShapeDtypeStruct((size, size), jnp.float32),
        scratch_shapes=[pltpu.VMEM((size, 2 * size), jnp.float32)],
        name="lower_inverse",
    )(corner)


def pick_kernel(index_ref, front_ref, out_ref):
    out_ref[0] = front_ref[...]


def pick_columns(index, front):
    rows = front.shape[0]
    count = index.shape[0]
    return pl.pallas_call(
        pick_kernel,
        out_shape=jax.ShapeDtypeStruct((count, rows, BLOCK), jnp.float32),
        grid_spec=pltpu.PrefetchScalarGridSpec(
            num_scalar_prefetch=1,
            grid=(count,),
            in_specs=[pl.BlockSpec((rows, BLOCK), lambda i, index: (0, index[i]))],
            out_specs=pl.BlockSpec((1, rows, BLOCK), lambda i, index: (i, 0, 0)),
        ),
        name="pick_columns",
    )(index, front)


def schur_kernel(slot_ref, live_ref, piece_ref, cols_ref, factor_ref, inverse_ref, block_ref, out_ref, tmp):
    @pl.when(live_ref[pl.program_id(0)] > 0)
    def _():
        block = matmul_nt(block_ref[0], inverse_ref[...])
        tmp[...] = cols_ref[0] - matmul_nt(factor_ref[...], block)
        for dest in range(out_ref.shape[0]):
            start = pl.multiple_of(piece_ref[dest] * BLOCK, BLOCK)
            out_ref[dest] = tmp[pl.ds(start, BLOCK), :]


def schur_pieces(slot, live, piece, cols, factor, inverse, blocks):
    leaves = slot.shape[0]
    bands = piece.shape[0]
    rows, panel = factor.shape
    return pl.pallas_call(
        schur_kernel,
        out_shape=jax.ShapeDtypeStruct((leaves * bands, BLOCK, BLOCK), jnp.float32),
        grid_spec=pltpu.PrefetchScalarGridSpec(
            num_scalar_prefetch=3,
            grid=(leaves,),
            in_specs=[
                pl.BlockSpec((1, rows, BLOCK), lambda i, s, v, p: (s[i], 0, 0)),
                pl.BlockSpec((rows, panel), lambda i, s, v, p: (0, 0)),
                pl.BlockSpec((panel, panel), lambda i, s, v, p: (0, 0)),
                pl.BlockSpec((1, BLOCK, panel), lambda i, s, v, p: (s[i], 0, 0)),
            ],
            out_specs=pl.BlockSpec((bands, BLOCK, BLOCK), lambda i, s, v, p: (i, 0, 0)),
            scratch_shapes=[pltpu.VMEM((rows, BLOCK), jnp.float32)],
        ),
        name="schur_pieces",
    )(slot, live, piece, cols, factor, inverse, blocks)


def place_kernel(slot_ref, parent_ref, blocks_ref, out_ref):
    step = pl.program_id(0)

    @pl.when(step == 0)
    def _():
        out_ref[...] = parent_ref[...]

    count = blocks_ref.shape[0]
    for item in range(count):
        slot = slot_ref[step * count + item]

        @pl.when(slot >= 0)
        def _(item=item, slot=slot):
            start = pl.multiple_of(slot * BLOCK, BLOCK)
            out_ref[pl.ds(start, BLOCK), :] += blocks_ref[item]


def place_blocks(slots, parent, blocks):
    total = blocks.shape[0]
    batch = 8
    rows = parent.shape[0]
    return pl.pallas_call(
        place_kernel,
        out_shape=jax.ShapeDtypeStruct(parent.shape, jnp.float32),
        grid_spec=pltpu.PrefetchScalarGridSpec(
            num_scalar_prefetch=1,
            grid=(total // batch,),
            in_specs=[
                pl.BlockSpec((rows, BLOCK), lambda i, slots: (0, 0)),
                pl.BlockSpec((batch, BLOCK, BLOCK), lambda i, slots: (i, 0, 0)),
            ],
            out_specs=pl.BlockSpec((rows, BLOCK), lambda i, slots: (0, 0)),
        ),
        name="place_blocks",
    )(slots, parent, blocks)


def locate(values, usable, count):
    hit = (values[..., None, :] == jnp.arange(count)[:, None]) & usable[..., None, :]
    index = jnp.sum(jnp.where(hit, jnp.arange(values.shape[-1]), 0), axis=-1)
    return index.astype(jnp.int32), jnp.any(hit, axis=-1)


def at(value, index, axis=0):
    return lax.dynamic_index_in_dim(value, index, axis, keepdims=False)


def gather_col(value):
    along = spread(value, "col_0", lax.axis_size("col_0"))
    other = lax.ppermute(along, "col_1", [(0, 1), (1, 0)])
    first = lax.axis_index("col_1") == 0
    both = jnp.stack([jnp.where(first, along, other), jnp.where(first, other, along)], axis=1)
    return both.reshape(-1, *value.shape)


def side_by_side(blocks):
    return jnp.concatenate([blocks[i] for i in range(blocks.shape[0])], axis=1)


def per_device(child_front, parent_front, block_map):
    front = child_front[0]
    parent = parent_front[:, 0, 0, :]
    grid_rows = lax.axis_size("row")
    grid_cols = lax.axis_size(COL)
    leaves = lax.axis_size("leaf")
    row_id = lax.axis_index("row")
    col_id = lax.axis_index(COL)
    leaf_id = lax.axis_index("leaf")
    rows = front.shape[0]
    child_blocks = rows // BLOCK
    lead = PANEL // BLOCK
    parent_rows = parent.shape[0]

    padded = jnp.concatenate([jnp.full((leaves, lead), -1, jnp.int32), block_map], axis=1)
    maps = padded.reshape(leaves, grid_rows, child_blocks)
    usable = maps >= 0
    band = maps // grid_cols
    residue = maps % grid_cols
    lo_index, lo_valid = locate(residue, usable, grid_cols)
    hi_index, hi_valid = locate(band, usable, grid_rows)
    own_lo_index, own_lo_valid = at(lo_index, leaf_id), at(lo_valid, leaf_id)
    column_index = at(own_lo_index, col_id, 1)
    column_valid = at(own_lo_valid, col_id, 1)

    share = PANEL // grid_cols
    deals = front[:, :PANEL].reshape(-1, grid_cols, share, PANEL).transpose(1, 0, 2, 3)
    deal = exchange(deals.reshape(grid_cols, -1, PANEL), COL)[0]
    corner = gather_col(spread(deal[:share], "row", grid_rows)[0]).reshape(PANEL, PANEL)
    raw = gather_col(deal).reshape(grid_cols, -1, share, PANEL)
    raw = raw.transpose(1, 0, 2, 3).reshape(rows, PANEL)
    mine = lax.dynamic_slice_in_dim(raw, at(column_index, row_id) * BLOCK, BLOCK, 0)
    blocks = lax.all_gather(mine, "row")
    cols = exchange(pick_columns(at(own_lo_index, col_id), front), COL)
    inverse = lower_inverse(corner)
    factor = matmul_nt(raw, inverse)

    column_band = jnp.sum(
        jnp.where(jnp.arange(child_blocks) == column_index[:, None], at(band, leaf_id), 0), axis=-1
    )
    slot, slot_valid = locate(column_band, column_valid, leaves)
    pieces = schur_pieces(
        slot,
        slot_valid.astype(jnp.int32),
        at(at(hi_index, leaf_id), row_id),
        cols,
        factor,
        inverse,
        blocks,
    )

    own_column = leaf_id * grid_cols + col_id
    present = jnp.any((maps == own_column) & usable, axis=(1, 2))
    row_slot = jnp.sum(
        jnp.where(jnp.arange(child_blocks) == hi_index[..., None], residue[:, :, None, :], 0),
        axis=-1,
    )
    row_slot = jnp.where(hi_valid & present[:, None, None], row_slot, -1).astype(jnp.int32)

    tops = exchange(pieces.reshape(leaves, grid_rows, BLOCK, BLOCK)[:, 0], "leaf")
    top_slot = at(row_slot, row_id, 1)[:, 0]
    top = jnp.where(row_id == 0, parent[:PANEL], 0.0).reshape(lead, BLOCK, BLOCK)
    top = top + jnp.stack(
        [
            sum(jnp.where(top_slot[c] == i, tops[c], 0.0) for c in range(leaves))
            for i in range(lead)
        ]
    )
    top = jnp.sum(exchange(top.reshape(grid_rows, -1, BLOCK), "row"), axis=0)
    top = spread(top, "row", grid_rows).reshape(PANEL, BLOCK)
    arrived = exchange(pieces, LEAF_ROW)

    every_leaf = lax.all_gather(top, "leaf")
    pair = jnp.stack([at(every_leaf, row_id), every_leaf[0]])
    every_col = lax.all_gather(pair, COL)
    band_top = side_by_side(every_col[:, 0])
    inverse_parent = lower_inverse(side_by_side(every_col[:lead, 1]))
    band_upper = matmul(inverse_parent, band_top)
    upper = matmul(inverse_parent, top)
    global_row = row_id * parent_rows + jnp.arange(parent_rows)
    update = jnp.where((global_row < PANEL)[:, None], 0.0, matmul_tn(band_upper, upper))
    in_panel = own_column < lead
    start = jnp.minimum(own_column, lead - 1) * BLOCK
    panel = lax.dynamic_slice_in_dim(band_upper, start, BLOCK, 0).T
    base = jnp.where(in_panel, panel, parent - update)
    slots = jnp.where(in_panel, -1, at(row_slot, row_id, 2)).reshape(-1)
    result = place_blocks(slots, base, arrived)
    return (factor[None], result[:, None, None, :])


def solution(mesh):
    torus = Mesh(
        mesh.devices.reshape(mesh.shape["leaf"], mesh.shape["row"], 4, 2),
        ("leaf", "row", "col_0", "col_1"),
    )
    in_specs = (P("leaf", "row", COL), P("row", None, LEAF_COL, None), P())
    out_specs = (P("leaf", "row", None), P("row", None, LEAF_COL, None))
    return jax.shard_map(
        per_device, mesh=torus, in_specs=in_specs, out_specs=out_specs, check_vma=False
    )
```

```python
import jax
import jax.numpy as jnp
from jax import lax
from jax.experimental import pallas as pl
from jax.experimental.pallas import tpu as pltpu
from jax.sharding import Mesh
from jax.sharding import PartitionSpec as P

FP = 8192
PANEL = 256
BLOCK = 128
COL = ("col_0", "col_1")
LEAF_COL = ("leaf", "col_0", "col_1")
LEAF_ROW = ("leaf", "row")
HIGHEST = lax.Precision.HIGHEST
STEP = 64
GROUP = 8


def matmul(left, right):
    return jnp.dot(left, right, precision=HIGHEST, preferred_element_type=jnp.float32)


def matmul_nt(left, right):
    return lax.dot_general(
        left,
        right,
        (((1,), (1,)), ((), ())),
        precision=HIGHEST,
        preferred_element_type=jnp.float32,
    )


def matmul_tn(left, right):
    return lax.dot_general(
        left,
        right,
        (((0,), (0,)), ((), ())),
        precision=HIGHEST,
        preferred_element_type=jnp.float32,
    )


def exchange(value, axes):
    return lax.all_to_all(value, axes, split_axis=0, concat_axis=0, tiled=True)


def spread(value, axes, count):
    return exchange(jnp.broadcast_to(value[None], (count, *value.shape)), axes)


def eliminate(tile, eye, step):
    width = 2 * step
    row = lax.broadcasted_iota(jnp.int32, (step, width), 0)
    work = jnp.concatenate([tile, eye], axis=1)
    pivots = jnp.ones((step, width), jnp.float32)

    def tall(value):
        return jnp.concatenate([value] * (step // 8), axis=0)

    for first in range(0, step, GROUP):
        span = range(GROUP)
        cols = [
            jnp.broadcast_to(work[:, first + i : first + i + 1], (step, width)) for i in span
        ]
        rows = [jnp.broadcast_to(work[first + i : first + i + 1, :], (8, width)) for i in span]
        small = {}
        for i in span:
            for j in range(i, GROUP):
                small[i, j] = jnp.broadcast_to(cols[i][first + j : first + j + 1, :], (8, width))
        ratio = {}
        recip = []
        for i in span:
            recip.append(1.0 / small[i, i])
            for j in range(i + 1, GROUP):
                ratio[i, j] = small[i, j] * recip[i]
            for j in range(i + 1, GROUP):
                for k in range(j, GROUP):
                    small[j, k] = small[j, k] - ratio[i, j] * small[i, k]
        update = None
        for i in span:
            scaled = jnp.where(row > first + i, cols[i] * tall(recip[i]), 0.0)
            pivots = jnp.where(row == first + i, tall(small[i, i]), pivots)
            for j in range(i + 1, GROUP):
                cols[j] = cols[j] - cols[i] * tall(ratio[i, j])
                rows[j] = rows[j] - ratio[i, j] * rows[i]
            term = scaled * tall(rows[i])
            update = term if update is None else update + term
        work = work - update
    return work[:, step:width] * lax.rsqrt(pivots)[:, :step]


def invert(corner, out_ref, work_ref):
    size = corner.shape[0]
    step = STEP
    row = lax.broadcasted_iota(jnp.int32, (size, size), 0)
    col = lax.broadcasted_iota(jnp.int32, (size, size), 1)
    work_ref[:, :size] = corner
    work_ref[:, size:] = (row == col).astype(jnp.float32)
    small_row = lax.broadcasted_iota(jnp.int32, (step, step), 0)
    small_col = lax.broadcasted_iota(jnp.int32, (step, step), 1)
    eye = (small_row == small_col).astype(jnp.float32)
    for start in range(0, size, step):
        stop = start + step
        lead = eliminate(work_ref[start:stop, start:stop], eye, step)
        upper = matmul(lead, work_ref[start:stop, :])
        out_ref[start:stop, :] = upper[:, size:]
        if stop < size:
            work_ref[stop:, :] = work_ref[stop:, :] - matmul_tn(upper[:, stop:size], upper)


def inverse_kernel(corner_ref, out_ref, work_ref):
    invert(corner_ref[...], out_ref, work_ref)


def lower_inverse(corner):
    size = corner.shape[0]
    return pl.pallas_call(
        inverse_kernel,
        out_shape=jax.ShapeDtypeStruct((size, size), jnp.float32),
        scratch_shapes=[pltpu.VMEM((size, 2 * size), jnp.float32)],
        name="lower_inverse",
    )(corner)


def parent_kernel(where_ref, tops_ref, top_ref, parent_ref, out_ref, inverse_ref, work_ref):
    row_id, own_column = where_ref[0], where_ref[1]
    lead = PANEL // BLOCK
    blocks = tops_ref.shape[0]
    corner = jnp.concatenate([tops_ref[i, 1] for i in range(lead)], axis=1)
    invert(corner, inverse_ref, work_ref)

    @pl.when(own_column >= lead)
    def _():
        upper = matmul(inverse_ref[...], top_ref[...])

        def body(block, carry):
            part = pl.ds(pl.multiple_of(block * BLOCK, BLOCK), BLOCK)
            change = matmul_tn(matmul(inverse_ref[...], tops_ref[block, 0]), upper)
            first = (row_id == 0) & (block < lead)
            out_ref[part, :] = parent_ref[part, :] - jnp.where(first, 0.0, change)
            return carry

        lax.fori_loop(0, blocks, body, 0)

    @pl.when(own_column < lead)
    def _():
        start = pl.multiple_of(jnp.minimum(own_column, lead - 1) * BLOCK, BLOCK)
        rows = inverse_ref[pl.ds(start, BLOCK), :]

        def body(block, carry):
            part = pl.ds(pl.multiple_of(block * BLOCK, BLOCK), BLOCK)
            out_ref[part, :] = matmul(rows, tops_ref[block, 0]).T
            return carry

        lax.fori_loop(0, blocks, body, 0)


def parent_base(where, tops, top, parent):
    vmem = pl.BlockSpec(memory_space=pltpu.VMEM)
    return pl.pallas_call(
        parent_kernel,
        out_shape=jax.ShapeDtypeStruct(parent.shape, jnp.float32),
        in_specs=[pl.BlockSpec(memory_space=pltpu.SMEM), vmem, vmem, vmem],
        out_specs=vmem,
        scratch_shapes=[
            pltpu.VMEM((PANEL, PANEL), jnp.float32),
            pltpu.VMEM((PANEL, 2 * PANEL), jnp.float32),
        ],
        name="parent_base",
    )(where, tops, top, parent)


def pick_kernel(index_ref, front_ref, out_ref):
    out_ref[0] = front_ref[...]


def pick_columns(index, front):
    rows = front.shape[0]
    count = index.shape[0]
    return pl.pallas_call(
        pick_kernel,
        out_shape=jax.ShapeDtypeStruct((count, rows, BLOCK), jnp.float32),
        grid_spec=pltpu.PrefetchScalarGridSpec(
            num_scalar_prefetch=1,
            grid=(count,),
            in_specs=[pl.BlockSpec((rows, BLOCK), lambda i, index: (0, index[i]))],
            out_specs=pl.BlockSpec((1, rows, BLOCK), lambda i, index: (i, 0, 0)),
        ),
        name="pick_columns",
    )(index, front)


def schur_kernel(
    slot_ref, live_ref, piece_ref, valid_ref, cols_ref, factor_ref, inverse_ref, block_ref,
    out_ref, top_ref, tmp_ref, sems, top_sems,
):
    leaves = live_ref.shape[0]
    bands = valid_ref.shape[0]

    def copies(leaf, dest):
        start = pl.multiple_of(piece_ref[dest] * BLOCK, BLOCK)
        piece = tmp_ref.at[leaf, pl.ds(start, BLOCK), :]
        item = leaf * bands + dest
        yield pltpu.make_async_copy(piece, out_ref.at[item], sems.at[item])
        if dest == 0:
            yield pltpu.make_async_copy(piece, top_ref.at[leaf], top_sems.at[leaf])

    def each(leaf, act):
        for dest in range(bands):

            @pl.when(valid_ref[dest] > 0)
            def _(dest=dest):
                for copy in copies(leaf, dest):
                    act(copy)

    def start(leaf, carry):
        @pl.when(live_ref[leaf] > 0)
        def _():
            slot = slot_ref[leaf]
            block = matmul_nt(block_ref[slot], inverse_ref[...])
            tmp_ref[leaf] = cols_ref[slot] - matmul_nt(factor_ref[...], block)
            each(leaf, lambda copy: copy.start())

        return carry

    def finish(leaf, carry):
        @pl.when(live_ref[leaf] > 0)
        def _():
            each(leaf, lambda copy: copy.wait())

        return carry

    lax.fori_loop(0, leaves, start, 0)
    lax.fori_loop(0, leaves, finish, 0)


def schur_pieces(slot, live, piece, valid, cols, factor, inverse, blocks):
    leaves = slot.shape[0]
    bands = piece.shape[0]
    rows = factor.shape[0]
    smem = pl.BlockSpec(memory_space=pltpu.SMEM)
    vmem = pl.BlockSpec(memory_space=pltpu.VMEM)
    anywhere = pl.BlockSpec(memory_space=pl.ANY)
    return pl.pallas_call(
        schur_kernel,
        out_shape=(
            jax.ShapeDtypeStruct((leaves * bands, BLOCK, BLOCK), jnp.float32),
            jax.ShapeDtypeStruct((leaves, BLOCK, BLOCK), jnp.float32),
        ),
        in_specs=[smem] * 4 + [vmem] * 4,
        out_specs=(anywhere, anywhere),
        scratch_shapes=[
            pltpu.VMEM((leaves, rows, BLOCK), jnp.float32),
            pltpu.SemaphoreType.DMA((leaves * bands,)),
            pltpu.SemaphoreType.DMA((leaves,)),
        ],
        name="schur_pieces",
    )(slot, live, piece, valid, cols, factor, inverse, blocks)


def place_kernel(slot_ref, base_ref, blocks_ref, out_ref):
    out_ref[...] = base_ref[...]

    def body(item, carry):
        slot = slot_ref[item]

        @pl.when(slot >= 0)
        def _():
            start = pl.multiple_of(slot * BLOCK, BLOCK)
            out_ref[pl.ds(start, BLOCK), :] += blocks_ref[item]

        return carry

    lax.fori_loop(0, blocks_ref.shape[0], body, 0)


def place_blocks(slots, base, blocks):
    vmem = pl.BlockSpec(memory_space=pltpu.VMEM)
    return pl.pallas_call(
        place_kernel,
        out_shape=jax.ShapeDtypeStruct(base.shape, jnp.float32),
        in_specs=[pl.BlockSpec(memory_space=pltpu.SMEM), vmem, vmem],
        out_specs=vmem,
        name="place_blocks",
    )(slots, base, blocks)


def locate(values, usable, count):
    hit = (values[..., None, :] == jnp.arange(count)[:, None]) & usable[..., None, :]
    index = jnp.sum(jnp.where(hit, jnp.arange(values.shape[-1]), 0), axis=-1)
    return index.astype(jnp.int32), jnp.any(hit, axis=-1)


def at(value, index, axis=0):
    return lax.dynamic_index_in_dim(value, index, axis, keepdims=False)


def ordered(value, other, first):
    return jnp.concatenate([jnp.where(first, value, other), jnp.where(first, other, value)])


def swapped_core(along):
    other = lax.ppermute(along, "col_1", [(0, 1), (1, 0)])
    first = lax.axis_index("col_1") == 0
    both = jnp.stack([jnp.where(first, along, other), jnp.where(first, other, along)], axis=1)
    return both.reshape(-1, *along.shape[1:])


def gather_col_permuted(value):
    index = lax.axis_index("col_0")
    along = value[None]
    for bit in range(2):
        other = lax.ppermute(along, "col_0", [(i, i ^ (1 << bit)) for i in range(4)])
        along = ordered(along, other, (index >> bit) % 2 == 0)
    return swapped_core(along)


def from_first_row(value):
    index = lax.axis_index("row")
    stride = lax.axis_size("row") // 2
    while stride:
        pairs = [(i, i + stride) for i in range(0, lax.axis_size("row"), 2 * stride)]
        other = lax.ppermute(value, "row", pairs)
        value = jnp.where(index % (2 * stride) == stride, other, value)
        stride //= 2
    return value


def per_device(child_front, parent_front, block_map):
    front = child_front[0]
    parent = parent_front[:, 0, 0, :]
    grid_rows = lax.axis_size("row")
    grid_cols = lax.axis_size(COL)
    leaves = lax.axis_size("leaf")
    row_id = lax.axis_index("row")
    col_id = lax.axis_index(COL)
    leaf_id = lax.axis_index("leaf")
    rows = front.shape[0]
    child_blocks = rows // BLOCK
    lead = PANEL // BLOCK
    parent_rows = parent.shape[0]

    padded = jnp.concatenate([jnp.full((leaves, lead), -1, jnp.int32), block_map], axis=1)
    maps = padded.reshape(leaves, grid_rows, child_blocks)
    usable = maps >= 0
    band = maps // grid_cols
    residue = maps % grid_cols
    lo_index, lo_valid = locate(residue, usable, grid_cols)
    hi_index, hi_valid = locate(band, usable, grid_rows)
    own_lo_index, own_lo_valid = at(lo_index, leaf_id), at(lo_valid, leaf_id)
    column_index = at(own_lo_index, col_id, 1)
    column_valid = at(own_lo_valid, col_id, 1)

    share = PANEL // grid_cols
    deals = front[:, :PANEL].reshape(-1, grid_cols, share, PANEL).transpose(1, 0, 2, 3)
    deal = exchange(deals.reshape(grid_cols, -1, PANEL), COL)[0]
    corner = gather_col_permuted(from_first_row(deal[:share])).reshape(PANEL, PANEL)
    along = spread(deal, "col_0", lax.axis_size("col_0"))
    picked = pick_columns(at(own_lo_index, col_id), front)
    picked, along = lax.optimization_barrier((picked, along))
    raw = swapped_core(along).reshape(grid_cols, -1, share, PANEL)
    raw = raw.transpose(1, 0, 2, 3).reshape(rows, PANEL)
    mine = lax.dynamic_slice_in_dim(raw, at(column_index, row_id) * BLOCK, BLOCK, 0)
    blocks = lax.all_gather(mine, "row")
    cols = exchange(picked, COL)
    inverse = lower_inverse(corner)
    factor = matmul_nt(raw, inverse)

    column_band = jnp.sum(
        jnp.where(jnp.arange(child_blocks) == column_index[:, None], at(band, leaf_id), 0), axis=-1
    )
    slot, slot_valid = locate(column_band, column_valid, leaves)
    pieces, tops = schur_pieces(
        slot,
        slot_valid.astype(jnp.int32),
        at(at(hi_index, leaf_id), row_id),
        at(at(hi_valid, leaf_id), row_id).astype(jnp.int32),
        cols,
        factor,
        inverse,
        blocks,
    )

    own_column = leaf_id * grid_cols + col_id
    present = jnp.any((maps == own_column) & usable, axis=(1, 2))
    row_slot = jnp.sum(
        jnp.where(jnp.arange(child_blocks) == hi_index[..., None], residue[:, :, None, :], 0),
        axis=-1,
    )
    row_slot = jnp.where(hi_valid & present[:, None, None], row_slot, -1).astype(jnp.int32)

    tops = exchange(tops, "leaf")
    top_slot = at(row_slot, row_id, 1)[:, 0]
    top = jnp.where(row_id == 0, parent[:PANEL], 0.0).reshape(lead, BLOCK, BLOCK)
    top = top + jnp.stack(
        [
            sum(jnp.where(top_slot[c] == i, tops[c], 0.0) for c in range(leaves))
            for i in range(lead)
        ]
    )
    top = jnp.sum(exchange(top.reshape(grid_rows, -1, BLOCK), "row"), axis=0)
    top = spread(top, "row", grid_rows).reshape(PANEL, BLOCK)
    arrived = exchange(pieces, LEAF_ROW)

    every_leaf = lax.all_gather(top, "leaf")
    pair = jnp.stack([at(every_leaf, row_id), every_leaf[0]])
    every_col = lax.all_gather(pair, COL)
    base = parent_base(jnp.stack([row_id, own_column]).astype(jnp.int32), every_col, top, parent)
    slots = jnp.where(own_column < lead, -1, at(row_slot, row_id, 2)).reshape(-1)
    result = place_blocks(slots, base, arrived)
    return (factor[None], result[:, None, None, :])


def solution(mesh):
    torus = Mesh(
        mesh.devices.reshape(mesh.shape["leaf"], mesh.shape["row"], 4, 2),
        ("leaf", "row", "col_0", "col_1"),
    )
    in_specs = (P("leaf", "row", COL), P("row", None, LEAF_COL, None), P())
    out_specs = (P("leaf", "row", None), P("row", None, LEAF_COL, None))
    return jax.shard_map(
        per_device, mesh=torus, in_specs=in_specs, out_specs=out_specs, check_vma=False
    )
```

```python
import jax
import jax.numpy as jnp
from jax import lax
from jax.experimental import pallas as pl
from jax.experimental.pallas import tpu as pltpu
from jax.sharding import Mesh
from jax.sharding import PartitionSpec as P

FP = 8192
PANEL = 256
BLOCK = 128
COL = ("col_0", "col_1")
LEAF_COL = ("leaf", "col_0", "col_1")
LEAF_ROW = ("leaf", "row")
HIGHEST = lax.Precision.HIGHEST
STEP = 64
GROUP = 8


def matmul(left, right):
    return jnp.dot(left, right, precision=HIGHEST, preferred_element_type=jnp.float32)


def matmul_nt(left, right):
    return lax.dot_general(
        left,
        right,
        (((1,), (1,)), ((), ())),
        precision=HIGHEST,
        preferred_element_type=jnp.float32,
    )


def matmul_tn(left, right):
    return lax.dot_general(
        left,
        right,
        (((0,), (0,)), ((), ())),
        precision=HIGHEST,
        preferred_element_type=jnp.float32,
    )


def exchange(value, axes):
    return lax.all_to_all(value, axes, split_axis=0, concat_axis=0, tiled=True)


def spread(value, axes, count):
    return exchange(jnp.broadcast_to(value[None], (count, *value.shape)), axes)


def eliminate(tile, eye, step):
    width = 2 * step
    row = lax.broadcasted_iota(jnp.int32, (step, width), 0)
    work = jnp.concatenate([tile, eye], axis=1)
    pivots = jnp.ones((step, width), jnp.float32)

    def tall(value):
        return jnp.concatenate([value] * (step // 8), axis=0)

    for first in range(0, step, GROUP):
        span = range(GROUP)
        cols = [
            jnp.broadcast_to(work[:, first + i : first + i + 1], (step, width)) for i in span
        ]
        rows = [jnp.broadcast_to(work[first + i : first + i + 1, :], (8, width)) for i in span]
        small = {}
        for i in span:
            for j in range(i, GROUP):
                small[i, j] = jnp.broadcast_to(cols[i][first + j : first + j + 1, :], (8, width))
        ratio = {}
        recip = []
        for i in span:
            recip.append(1.0 / small[i, i])
            for j in range(i + 1, GROUP):
                ratio[i, j] = small[i, j] * recip[i]
            for j in range(i + 1, GROUP):
                for k in range(j, GROUP):
                    small[j, k] = small[j, k] - ratio[i, j] * small[i, k]
        update = None
        for i in span:
            scaled = jnp.where(row > first + i, cols[i] * tall(recip[i]), 0.0)
            pivots = jnp.where(row == first + i, tall(small[i, i]), pivots)
            for j in range(i + 1, GROUP):
                cols[j] = cols[j] - cols[i] * tall(ratio[i, j])
                rows[j] = rows[j] - ratio[i, j] * rows[i]
            term = scaled * tall(rows[i])
            update = term if update is None else update + term
        work = work - update
    return work[:, step:width] * lax.rsqrt(pivots)[:, :step]


def invert(corner, out_ref, work_ref):
    size = corner.shape[0]
    step = STEP
    row = lax.broadcasted_iota(jnp.int32, (size, size), 0)
    col = lax.broadcasted_iota(jnp.int32, (size, size), 1)
    work_ref[:, :size] = corner
    work_ref[:, size:] = (row == col).astype(jnp.float32)
    small_row = lax.broadcasted_iota(jnp.int32, (step, step), 0)
    small_col = lax.broadcasted_iota(jnp.int32, (step, step), 1)
    eye = (small_row == small_col).astype(jnp.float32)
    for start in range(0, size, step):
        stop = start + step
        lead = eliminate(work_ref[start:stop, start:stop], eye, step)
        upper = matmul(lead, work_ref[start:stop, :])
        out_ref[start:stop, :] = upper[:, size:]
        if stop < size:
            work_ref[stop:, :] = work_ref[stop:, :] - matmul_tn(upper[:, stop:size], upper)


def inverse_kernel(corner_ref, out_ref, work_ref):
    invert(corner_ref[...], out_ref, work_ref)


def lower_inverse(corner):
    size = corner.shape[0]
    return pl.pallas_call(
        inverse_kernel,
        out_shape=jax.ShapeDtypeStruct((size, size), jnp.float32),
        scratch_shapes=[pltpu.VMEM((size, 2 * size), jnp.float32)],
        name="lower_inverse",
    )(corner)


def parent_kernel(where_ref, tops_ref, top_ref, parent_ref, out_ref, inverse_ref, work_ref):
    row_id, own_column = where_ref[0], where_ref[1]
    lead = PANEL // BLOCK
    blocks = tops_ref.shape[0]
    corner = jnp.concatenate([tops_ref[i, 1] for i in range(lead)], axis=1)
    invert(corner, inverse_ref, work_ref)

    @pl.when(own_column >= lead)
    def _():
        upper = matmul(inverse_ref[...], top_ref[...])

        def body(block, carry):
            part = pl.ds(pl.multiple_of(block * BLOCK, BLOCK), BLOCK)
            change = matmul_tn(matmul(inverse_ref[...], tops_ref[block, 0]), upper)
            first = (row_id == 0) & (block < lead)
            out_ref[part, :] = parent_ref[part, :] - jnp.where(first, 0.0, change)
            return carry

        lax.fori_loop(0, blocks, body, 0)

    @pl.when(own_column < lead)
    def _():
        start = pl.multiple_of(jnp.minimum(own_column, lead - 1) * BLOCK, BLOCK)
        rows = inverse_ref[pl.ds(start, BLOCK), :]

        def body(block, carry):
            part = pl.ds(pl.multiple_of(block * BLOCK, BLOCK), BLOCK)
            out_ref[part, :] = matmul(rows, tops_ref[block, 0]).T
            return carry

        lax.fori_loop(0, blocks, body, 0)


def parent_base(where, tops, top, parent):
    vmem = pl.BlockSpec(memory_space=pltpu.VMEM)
    return pl.pallas_call(
        parent_kernel,
        out_shape=jax.ShapeDtypeStruct(parent.shape, jnp.float32),
        in_specs=[pl.BlockSpec(memory_space=pltpu.SMEM), vmem, vmem, vmem],
        out_specs=vmem,
        scratch_shapes=[
            pltpu.VMEM((PANEL, PANEL), jnp.float32),
            pltpu.VMEM((PANEL, 2 * PANEL), jnp.float32),
        ],
        name="parent_base",
    )(where, tops, top, parent)


def pick_kernel(index_ref, front_ref, out_ref):
    out_ref[0] = front_ref[...]


def pick_columns(index, front):
    rows = front.shape[0]
    count = index.shape[0]
    return pl.pallas_call(
        pick_kernel,
        out_shape=jax.ShapeDtypeStruct((count, rows, BLOCK), jnp.float32),
        grid_spec=pltpu.PrefetchScalarGridSpec(
            num_scalar_prefetch=1,
            grid=(count,),
            in_specs=[pl.BlockSpec((rows, BLOCK), lambda i, index: (0, index[i]))],
            out_specs=pl.BlockSpec((1, rows, BLOCK), lambda i, index: (i, 0, 0)),
        ),
        name="pick_columns",
    )(index, front)


def schur_kernel(
    slot_ref, live_ref, piece_ref, valid_ref, cols_ref, factor_ref, inverse_ref, block_ref,
    out_ref, top_ref, tmp_ref, sems, top_sems,
):
    leaves = live_ref.shape[0]
    bands = valid_ref.shape[0]

    def copies(leaf, dest):
        start = pl.multiple_of(piece_ref[dest] * BLOCK, BLOCK)
        piece = tmp_ref.at[leaf, pl.ds(start, BLOCK), :]
        item = leaf * bands + dest
        yield pltpu.make_async_copy(piece, out_ref.at[item], sems.at[item])
        if dest == 0:
            yield pltpu.make_async_copy(piece, top_ref.at[leaf], top_sems.at[leaf])

    def each(leaf, act):
        for dest in range(bands):

            @pl.when(valid_ref[dest] > 0)
            def _(dest=dest):
                for copy in copies(leaf, dest):
                    act(copy)

    def start(leaf, carry):
        @pl.when(live_ref[leaf] > 0)
        def _():
            slot = slot_ref[leaf]
            block = matmul_nt(block_ref[slot], inverse_ref[...])
            tmp_ref[leaf] = cols_ref[slot] - matmul_nt(factor_ref[...], block)
            each(leaf, lambda copy: copy.start())

        return carry

    def finish(leaf, carry):
        @pl.when(live_ref[leaf] > 0)
        def _():
            each(leaf, lambda copy: copy.wait())

        return carry

    lax.fori_loop(0, leaves, start, 0)
    lax.fori_loop(0, leaves, finish, 0)


def schur_pieces(slot, live, piece, valid, cols, factor, inverse, blocks):
    leaves = slot.shape[0]
    bands = piece.shape[0]
    rows = factor.shape[0]
    smem = pl.BlockSpec(memory_space=pltpu.SMEM)
    vmem = pl.BlockSpec(memory_space=pltpu.VMEM)
    anywhere = pl.BlockSpec(memory_space=pl.ANY)
    return pl.pallas_call(
        schur_kernel,
        out_shape=(
            jax.ShapeDtypeStruct((leaves * bands, BLOCK, BLOCK), jnp.float32),
            jax.ShapeDtypeStruct((leaves, BLOCK, BLOCK), jnp.float32),
        ),
        in_specs=[smem] * 4 + [vmem] * 4,
        out_specs=(anywhere, anywhere),
        scratch_shapes=[
            pltpu.VMEM((leaves, rows, BLOCK), jnp.float32),
            pltpu.SemaphoreType.DMA((leaves * bands,)),
            pltpu.SemaphoreType.DMA((leaves,)),
        ],
        name="schur_pieces",
    )(slot, live, piece, valid, cols, factor, inverse, blocks)


def place_kernel(slot_ref, base_ref, blocks_ref, out_ref):
    out_ref[...] = base_ref[...]

    def body(item, carry):
        slot = slot_ref[item]

        @pl.when(slot >= 0)
        def _():
            start = pl.multiple_of(slot * BLOCK, BLOCK)
            out_ref[pl.ds(start, BLOCK), :] += blocks_ref[item]

        return carry

    lax.fori_loop(0, blocks_ref.shape[0], body, 0)


def place_blocks(slots, base, blocks):
    vmem = pl.BlockSpec(memory_space=pltpu.VMEM)
    return pl.pallas_call(
        place_kernel,
        out_shape=jax.ShapeDtypeStruct(base.shape, jnp.float32),
        in_specs=[pl.BlockSpec(memory_space=pltpu.SMEM), vmem, vmem],
        out_specs=vmem,
        name="place_blocks",
    )(slots, base, blocks)


def locate(values, usable, count):
    hit = (values[..., None, :] == jnp.arange(count)[:, None]) & usable[..., None, :]
    index = jnp.sum(jnp.where(hit, jnp.arange(values.shape[-1]), 0), axis=-1)
    return index.astype(jnp.int32), jnp.any(hit, axis=-1)


def at(value, index, axis=0):
    return lax.dynamic_index_in_dim(value, index, axis, keepdims=False)


def swapped_core(along):
    other = lax.ppermute(along, "col_1", [(0, 1), (1, 0)])
    first = lax.axis_index("col_1") == 0
    both = jnp.stack([jnp.where(first, along, other), jnp.where(first, other, along)], axis=1)
    return both.reshape(-1, *along.shape[1:])


def from_first_row(value):
    index = lax.axis_index("row")
    stride = lax.axis_size("row") // 2
    while stride:
        pairs = [(i, i + stride) for i in range(0, lax.axis_size("row"), 2 * stride)]
        other = lax.ppermute(value, "row", pairs)
        value = jnp.where(index % (2 * stride) == stride, other, value)
        stride //= 2
    return value


def per_device(child_front, parent_front, block_map):
    front = child_front[0]
    parent = parent_front[:, 0, 0, :]
    grid_rows = lax.axis_size("row")
    grid_cols = lax.axis_size(COL)
    leaves = lax.axis_size("leaf")
    row_id = lax.axis_index("row")
    col_id = lax.axis_index(COL)
    leaf_id = lax.axis_index("leaf")
    rows = front.shape[0]
    child_blocks = rows // BLOCK
    lead = PANEL // BLOCK
    parent_rows = parent.shape[0]

    padded = jnp.concatenate([jnp.full((leaves, lead), -1, jnp.int32), block_map], axis=1)
    maps = padded.reshape(leaves, grid_rows, child_blocks)
    usable = maps >= 0
    band = maps // grid_cols
    residue = maps % grid_cols
    lo_index, lo_valid = locate(residue, usable, grid_cols)
    hi_index, hi_valid = locate(band, usable, grid_rows)
    own_lo_index, own_lo_valid = at(lo_index, leaf_id), at(lo_valid, leaf_id)
    column_index = at(own_lo_index, col_id, 1)
    column_valid = at(own_lo_valid, col_id, 1)

    parent_top = lax.all_gather(parent[:PANEL], "row")[0]
    share = PANEL // grid_cols
    deals = front[:, :PANEL].reshape(-1, grid_cols, share, PANEL).transpose(1, 0, 2, 3)
    deal = exchange(deals.reshape(grid_cols, -1, PANEL), COL)[0]
    along = spread(deal, "col_0", lax.axis_size("col_0"))
    corner = spread(from_first_row(deal[:share]), "col_0", lax.axis_size("col_0"))
    picked = pick_columns(at(own_lo_index, col_id), front)
    raw = swapped_core(along).reshape(grid_cols, -1, share, PANEL)
    raw = raw.transpose(1, 0, 2, 3).reshape(rows, PANEL)
    mine = lax.dynamic_slice_in_dim(raw, at(column_index, row_id) * BLOCK, BLOCK, 0)
    mine, parent_top = lax.optimization_barrier((mine, parent_top))
    blocks = lax.all_gather(mine, "row")
    picked, corner, mine = lax.optimization_barrier((picked, corner, mine))
    corner = swapped_core(corner).reshape(PANEL, PANEL)
    cols = exchange(picked, COL)
    inverse = lower_inverse(corner)
    factor = matmul_nt(raw, inverse)

    column_band = jnp.sum(
        jnp.where(jnp.arange(child_blocks) == column_index[:, None], at(band, leaf_id), 0), axis=-1
    )
    slot, slot_valid = locate(column_band, column_valid, leaves)
    pieces, tops = schur_pieces(
        slot,
        slot_valid.astype(jnp.int32),
        at(at(hi_index, leaf_id), row_id),
        at(at(hi_valid, leaf_id), row_id).astype(jnp.int32),
        cols,
        factor,
        inverse,
        blocks,
    )

    own_column = leaf_id * grid_cols + col_id
    present = jnp.any((maps == own_column) & usable, axis=(1, 2))
    row_slot = jnp.sum(
        jnp.where(jnp.arange(child_blocks) == hi_index[..., None], residue[:, :, None, :], 0),
        axis=-1,
    )
    row_slot = jnp.where(hi_valid & present[:, None, None], row_slot, -1).astype(jnp.int32)

    tops = exchange(tops.reshape(leaves * grid_rows, -1, BLOCK), LEAF_ROW)
    chosen = row_slot[:, :, 0].reshape(-1) == jnp.arange(lead)[:, None]
    top = jnp.sum(jnp.where(chosen[:, :, None, None], tops, 0.0), axis=1)
    top = spread(top, "row", grid_rows).transpose(1, 0, 2, 3).reshape(PANEL, BLOCK) + parent_top
    arrived = exchange(pieces, LEAF_ROW)

    every_leaf = lax.all_gather(top, "leaf")
    pair = jnp.stack([at(every_leaf, row_id), every_leaf[0]])
    every_col = lax.all_gather(pair, COL)
    base = parent_base(jnp.stack([row_id, own_column]).astype(jnp.int32), every_col, top, parent)
    slots = jnp.where(own_column < lead, -1, at(row_slot, row_id, 2)).reshape(-1)
    result = place_blocks(slots, base, arrived)
    return (factor[None], result[:, None, None, :])


def solution(mesh):
    torus = Mesh(
        mesh.devices.reshape(mesh.shape["leaf"], mesh.shape["row"], 4, 2),
        ("leaf", "row", "col_0", "col_1"),
    )
    in_specs = (P("leaf", "row", COL), P("row", None, LEAF_COL, None), P())
    out_specs = (P("leaf", "row", None), P("row", None, LEAF_COL, None))
    return jax.shard_map(
        per_device, mesh=torus, in_specs=in_specs, out_specs=out_specs, check_vma=False
    )
```

```python
import jax
import jax.numpy as jnp
from jax import lax
from jax.experimental import pallas as pl
from jax.experimental.pallas import tpu as pltpu
from jax.sharding import Mesh
from jax.sharding import PartitionSpec as P

FP = 8192
PANEL = 256
BLOCK = 128
COL = ("col_0", "col_1")
LEAF_COL = ("leaf", "col_0", "col_1")
LEAF_ROW = ("leaf", "row")
HIGHEST = lax.Precision.HIGHEST
STEP = 64
GROUP = 8


def matmul(left, right):
    return jnp.dot(left, right, precision=HIGHEST, preferred_element_type=jnp.float32)


def matmul_nt(left, right):
    return lax.dot_general(
        left,
        right,
        (((1,), (1,)), ((), ())),
        precision=HIGHEST,
        preferred_element_type=jnp.float32,
    )


def matmul_tn(left, right):
    return lax.dot_general(
        left,
        right,
        (((0,), (0,)), ((), ())),
        precision=HIGHEST,
        preferred_element_type=jnp.float32,
    )


def exchange(value, axes):
    return lax.all_to_all(value, axes, split_axis=0, concat_axis=0, tiled=True)


def spread(value, axes, count):
    return exchange(jnp.broadcast_to(value[None], (count, *value.shape)), axes)


def eliminate(tile, eye, step):
    width = 2 * step
    row = lax.broadcasted_iota(jnp.int32, (step, width), 0)
    work = jnp.concatenate([tile, eye], axis=1)
    pivots = jnp.ones((step, width), jnp.float32)

    def tall(value):
        return jnp.concatenate([value] * (step // 8), axis=0)

    for first in range(0, step, GROUP):
        span = range(GROUP)
        cols = [
            jnp.broadcast_to(work[:, first + i : first + i + 1], (step, width)) for i in span
        ]
        rows = [jnp.broadcast_to(work[first + i : first + i + 1, :], (8, width)) for i in span]
        small = {}
        for i in span:
            for j in range(i, GROUP):
                small[i, j] = jnp.broadcast_to(cols[i][first + j : first + j + 1, :], (8, width))
        ratio = {}
        recip = []
        for i in span:
            recip.append(1.0 / small[i, i])
            for j in range(i + 1, GROUP):
                ratio[i, j] = small[i, j] * recip[i]
            for j in range(i + 1, GROUP):
                for k in range(j, GROUP):
                    small[j, k] = small[j, k] - ratio[i, j] * small[i, k]
        update = None
        for i in span:
            scaled = jnp.where(row > first + i, cols[i] * tall(recip[i]), 0.0)
            pivots = jnp.where(row == first + i, tall(small[i, i]), pivots)
            for j in range(i + 1, GROUP):
                cols[j] = cols[j] - cols[i] * tall(ratio[i, j])
                rows[j] = rows[j] - ratio[i, j] * rows[i]
            term = scaled * tall(rows[i])
            update = term if update is None else update + term
        work = work - update
    return work[:, step:width] * lax.rsqrt(pivots)[:, :step]


def invert(corner, out_ref, work_ref):
    size = corner.shape[0]
    step = STEP
    row = lax.broadcasted_iota(jnp.int32, (size, size), 0)
    col = lax.broadcasted_iota(jnp.int32, (size, size), 1)
    work_ref[:, :size] = corner
    work_ref[:, size:] = (row == col).astype(jnp.float32)
    small_row = lax.broadcasted_iota(jnp.int32, (step, step), 0)
    small_col = lax.broadcasted_iota(jnp.int32, (step, step), 1)
    eye = (small_row == small_col).astype(jnp.float32)
    for start in range(0, size, step):
        stop = start + step
        lead = eliminate(work_ref[start:stop, start:stop], eye, step)
        upper = matmul(lead, work_ref[start:stop, :])
        out_ref[start:stop, :] = upper[:, size:]
        if stop < size:
            work_ref[stop:, :] = work_ref[stop:, :] - matmul_tn(upper[:, stop:size], upper)


def inverse_kernel(corner_ref, out_ref, work_ref):
    invert(corner_ref[...], out_ref, work_ref)


def lower_inverse(corner):
    size = corner.shape[0]
    return pl.pallas_call(
        inverse_kernel,
        out_shape=jax.ShapeDtypeStruct((size, size), jnp.float32),
        scratch_shapes=[pltpu.VMEM((size, 2 * size), jnp.float32)],
        name="lower_inverse",
    )(corner)


def parent_kernel(where_ref, inverse_ref, tops_ref, top_ref, parent_ref, out_ref):
    row_id, own_column = where_ref[0], where_ref[1]
    lead = PANEL // BLOCK
    blocks = tops_ref.shape[0]

    @pl.when(own_column >= lead)
    def _():
        upper = matmul(inverse_ref[...], top_ref[...])

        def body(block, carry):
            part = pl.ds(pl.multiple_of(block * BLOCK, BLOCK), BLOCK)
            change = matmul_tn(matmul(inverse_ref[...], tops_ref[block]), upper)
            first = (row_id == 0) & (block < lead)
            out_ref[part, :] = parent_ref[part, :] - jnp.where(first, 0.0, change)
            return carry

        lax.fori_loop(0, blocks, body, 0)

    @pl.when(own_column < lead)
    def _():
        start = pl.multiple_of(jnp.minimum(own_column, lead - 1) * BLOCK, BLOCK)
        rows = inverse_ref[pl.ds(start, BLOCK), :]

        def body(block, carry):
            part = pl.ds(pl.multiple_of(block * BLOCK, BLOCK), BLOCK)
            out_ref[part, :] = matmul(rows, tops_ref[block]).T
            return carry

        lax.fori_loop(0, blocks, body, 0)


def parent_base(where, inverse, tops, top, parent):
    vmem = pl.BlockSpec(memory_space=pltpu.VMEM)
    return pl.pallas_call(
        parent_kernel,
        out_shape=jax.ShapeDtypeStruct(parent.shape, jnp.float32),
        in_specs=[pl.BlockSpec(memory_space=pltpu.SMEM), vmem, vmem, vmem, vmem],
        out_specs=vmem,
        name="parent_base",
    )(where, inverse, tops, top, parent)


def pick_kernel(index_ref, front_ref, out_ref):
    out_ref[0] = front_ref[...]


def pick_columns(index, front):
    rows = front.shape[0]
    count = index.shape[0]
    return pl.pallas_call(
        pick_kernel,
        out_shape=jax.ShapeDtypeStruct((count, rows, BLOCK), jnp.float32),
        grid_spec=pltpu.PrefetchScalarGridSpec(
            num_scalar_prefetch=1,
            grid=(count,),
            in_specs=[pl.BlockSpec((rows, BLOCK), lambda i, index: (0, index[i]))],
            out_specs=pl.BlockSpec((1, rows, BLOCK), lambda i, index: (i, 0, 0)),
        ),
        name="pick_columns",
    )(index, front)


def schur_kernel(
    slot_ref, live_ref, piece_ref, valid_ref, cols_ref, factor_ref, inverse_ref, block_ref,
    out_ref, top_ref, tmp_ref, sems, top_sems,
):
    leaves = live_ref.shape[0]
    bands = valid_ref.shape[0]

    def copies(leaf, dest):
        start = pl.multiple_of(piece_ref[dest] * BLOCK, BLOCK)
        piece = tmp_ref.at[leaf, pl.ds(start, BLOCK), :]
        item = leaf * bands + dest
        yield pltpu.make_async_copy(piece, out_ref.at[item], sems.at[item])
        if dest == 0:
            yield pltpu.make_async_copy(piece, top_ref.at[leaf], top_sems.at[leaf])

    def each(leaf, act):
        for dest in range(bands):

            @pl.when(valid_ref[dest] > 0)
            def _(dest=dest):
                for copy in copies(leaf, dest):
                    act(copy)

    def start(leaf, carry):
        @pl.when(live_ref[leaf] > 0)
        def _():
            slot = slot_ref[leaf]
            block = matmul_nt(block_ref[slot], inverse_ref[...])
            tmp_ref[leaf] = cols_ref[slot] - matmul_nt(factor_ref[...], block)
            each(leaf, lambda copy: copy.start())

        return carry

    def finish(leaf, carry):
        @pl.when(live_ref[leaf] > 0)
        def _():
            each(leaf, lambda copy: copy.wait())

        return carry

    lax.fori_loop(0, leaves, start, 0)
    lax.fori_loop(0, leaves, finish, 0)


def schur_pieces(slot, live, piece, valid, cols, factor, inverse, blocks):
    leaves = slot.shape[0]
    bands = piece.shape[0]
    rows = factor.shape[0]
    smem = pl.BlockSpec(memory_space=pltpu.SMEM)
    vmem = pl.BlockSpec(memory_space=pltpu.VMEM)
    anywhere = pl.BlockSpec(memory_space=pl.ANY)
    return pl.pallas_call(
        schur_kernel,
        out_shape=(
            jax.ShapeDtypeStruct((leaves * bands, BLOCK, BLOCK), jnp.float32),
            jax.ShapeDtypeStruct((leaves, BLOCK, BLOCK), jnp.float32),
        ),
        in_specs=[smem] * 4 + [vmem] * 4,
        out_specs=(anywhere, anywhere),
        scratch_shapes=[
            pltpu.VMEM((leaves, rows, BLOCK), jnp.float32),
            pltpu.SemaphoreType.DMA((leaves * bands,)),
            pltpu.SemaphoreType.DMA((leaves,)),
        ],
        name="schur_pieces",
    )(slot, live, piece, valid, cols, factor, inverse, blocks)


def place_kernel(slot_ref, base_ref, blocks_ref, out_ref):
    out_ref[...] = base_ref[...]

    def body(item, carry):
        slot = slot_ref[item]

        @pl.when(slot >= 0)
        def _():
            start = pl.multiple_of(slot * BLOCK, BLOCK)
            out_ref[pl.ds(start, BLOCK), :] += blocks_ref[item]

        return carry

    lax.fori_loop(0, blocks_ref.shape[0], body, 0)


def place_blocks(slots, base, blocks):
    vmem = pl.BlockSpec(memory_space=pltpu.VMEM)
    return pl.pallas_call(
        place_kernel,
        out_shape=jax.ShapeDtypeStruct(base.shape, jnp.float32),
        in_specs=[pl.BlockSpec(memory_space=pltpu.SMEM), vmem, vmem],
        out_specs=vmem,
        name="place_blocks",
    )(slots, base, blocks)


def locate(values, usable, count):
    hit = (values[..., None, :] == jnp.arange(count)[:, None]) & usable[..., None, :]
    index = jnp.sum(jnp.where(hit, jnp.arange(values.shape[-1]), 0), axis=-1)
    return index.astype(jnp.int32), jnp.any(hit, axis=-1)


def at(value, index, axis=0):
    return lax.dynamic_index_in_dim(value, index, axis, keepdims=False)


def swapped_core(along):
    other = lax.ppermute(along, "col_1", [(0, 1), (1, 0)])
    first = lax.axis_index("col_1") == 0
    both = jnp.stack([jnp.where(first, along, other), jnp.where(first, other, along)], axis=1)
    return both.reshape(-1, *along.shape[1:])


def from_first(value, axis):
    index = lax.axis_index(axis)
    stride = lax.axis_size(axis) // 2
    while stride:
        pairs = [(i, i + stride) for i in range(0, lax.axis_size(axis), 2 * stride)]
        other = lax.ppermute(value, axis, pairs)
        value = jnp.where(index % (2 * stride) == stride, other, value)
        stride //= 2
    return value


def per_device(child_front, parent_front, block_map):
    front = child_front[0]
    parent = parent_front[:, 0, 0, :]
    grid_rows = lax.axis_size("row")
    grid_cols = lax.axis_size(COL)
    leaves = lax.axis_size("leaf")
    row_id = lax.axis_index("row")
    col_id = lax.axis_index(COL)
    leaf_id = lax.axis_index("leaf")
    rows = front.shape[0]
    child_blocks = rows // BLOCK
    lead = PANEL // BLOCK
    parent_rows = parent.shape[0]

    padded = jnp.concatenate([jnp.full((leaves, lead), -1, jnp.int32), block_map], axis=1)
    maps = padded.reshape(leaves, grid_rows, child_blocks)
    usable = maps >= 0
    band = maps // grid_cols
    residue = maps % grid_cols
    lo_index, lo_valid = locate(residue, usable, grid_cols)
    hi_index, hi_valid = locate(band, usable, grid_rows)
    own_lo_index, own_lo_valid = at(lo_index, leaf_id), at(lo_valid, leaf_id)
    column_index = at(own_lo_index, col_id, 1)
    column_valid = at(own_lo_valid, col_id, 1)

    share = PANEL // grid_cols
    deals = front[:, :PANEL].reshape(-1, grid_cols, share, PANEL).transpose(1, 0, 2, 3)
    deal = exchange(deals.reshape(grid_cols, -1, PANEL), COL)[0]
    picked = pick_columns(at(own_lo_index, col_id), front)
    deal, picked = lax.optimization_barrier((deal, picked))
    along = spread(deal, "col_0", lax.axis_size("col_0"))
    corner, along = lax.optimization_barrier((from_first(deal[:share], "row"), along))
    corner = spread(corner, "col_0", lax.axis_size("col_0"))
    raw = swapped_core(along).reshape(grid_cols, -1, share, PANEL)
    raw = raw.transpose(1, 0, 2, 3).reshape(rows, PANEL)
    mine = lax.dynamic_slice_in_dim(raw, at(column_index, row_id) * BLOCK, BLOCK, 0)
    blocks = lax.all_gather(mine, "row")
    picked, corner, mine = lax.optimization_barrier((picked, corner, mine))
    corner = swapped_core(corner).reshape(PANEL, PANEL)
    cols = exchange(picked, COL)
    inverse = lower_inverse(corner)
    parent_top, inverse = lax.optimization_barrier((parent[:PANEL], inverse))
    parent_top = from_first(parent_top, "row")
    cols, parent_top = lax.optimization_barrier((cols, parent_top))
    factor = matmul_nt(raw, inverse)

    column_band = jnp.sum(
        jnp.where(jnp.arange(child_blocks) == column_index[:, None], at(band, leaf_id), 0), axis=-1
    )
    slot, slot_valid = locate(column_band, column_valid, leaves)
    pieces, tops = schur_pieces(
        slot,
        slot_valid.astype(jnp.int32),
        at(at(hi_index, leaf_id), row_id),
        at(at(hi_valid, leaf_id), row_id).astype(jnp.int32),
        cols,
        factor,
        inverse,
        blocks,
    )

    own_column = leaf_id * grid_cols + col_id
    present = jnp.any((maps == own_column) & usable, axis=(1, 2))
    row_slot = jnp.sum(
        jnp.where(jnp.arange(child_blocks) == hi_index[..., None], residue[:, :, None, :], 0),
        axis=-1,
    )
    row_slot = jnp.where(hi_valid & present[:, None, None], row_slot, -1).astype(jnp.int32)

    tops = exchange(tops.reshape(leaves * grid_rows, -1, BLOCK), LEAF_ROW)
    chosen = row_slot[:, :, 0].reshape(-1) == jnp.arange(lead)[:, None]
    top = jnp.sum(jnp.where(chosen[:, :, None, None], tops, 0.0), axis=1)
    top = spread(top, "row", grid_rows).transpose(1, 0, 2, 3).reshape(PANEL, BLOCK) + parent_top
    arrived = exchange(pieces, LEAF_ROW)

    every_leaf = lax.all_gather(top, "leaf")
    tops = lax.all_gather(at(every_leaf, row_id), COL)
    corner = from_first(every_leaf[0], "col_0")
    corner = lower_inverse(jnp.concatenate(list(swapped_core(corner[None])), axis=1))
    place = jnp.stack([row_id, own_column]).astype(jnp.int32)
    base = parent_base(place, corner, tops, top, parent)
    slots = jnp.where(own_column < lead, -1, at(row_slot, row_id, 2)).reshape(-1)
    result = place_blocks(slots, base, arrived)
    return (factor[None], result[:, None, None, :])


def solution(mesh):
    torus = Mesh(
        mesh.devices.reshape(mesh.shape["leaf"], mesh.shape["row"], 4, 2),
        ("leaf", "row", "col_0", "col_1"),
    )
    in_specs = (P("leaf", "row", COL), P("row", None, LEAF_COL, None), P())
    out_specs = (P("leaf", "row", None), P("row", None, LEAF_COL, None))
    return jax.shard_map(
        per_device, mesh=torus, in_specs=in_specs, out_specs=out_specs, check_vma=False
    )
```

```python
import jax
import jax.numpy as jnp
from jax import lax
from jax.experimental import pallas as pl
from jax.experimental.pallas import tpu as pltpu
from jax.sharding import Mesh
from jax.sharding import PartitionSpec as P

FP = 8192
PANEL = 256
BLOCK = 128
COL = ("col_0", "col_1")
LEAF_COL = ("leaf", "col_0", "col_1")
LEAF_ROW = ("leaf", "row")
HIGHEST = lax.Precision.HIGHEST
STEP = 64
GROUP = 8


def matmul(left, right):
    return jnp.dot(left, right, precision=HIGHEST, preferred_element_type=jnp.float32)


def matmul_nt(left, right):
    return lax.dot_general(
        left,
        right,
        (((1,), (1,)), ((), ())),
        precision=HIGHEST,
        preferred_element_type=jnp.float32,
    )


def matmul_tn(left, right):
    return lax.dot_general(
        left,
        right,
        (((0,), (0,)), ((), ())),
        precision=HIGHEST,
        preferred_element_type=jnp.float32,
    )


def exchange(value, axes):
    return lax.all_to_all(value, axes, split_axis=0, concat_axis=0, tiled=True)


def spread(value, axes, count):
    return exchange(jnp.broadcast_to(value[None], (count, *value.shape)), axes)


def eliminate(tile, eye, step):
    width = 2 * step
    row = lax.broadcasted_iota(jnp.int32, (step, width), 0)
    work = jnp.concatenate([tile, eye], axis=1)
    pivots = jnp.ones((step, width), jnp.float32)

    def tall(value):
        return jnp.concatenate([value] * (step // 8), axis=0)

    for first in range(0, step, GROUP):
        span = range(GROUP)
        cols = [
            jnp.broadcast_to(work[:, first + i : first + i + 1], (step, width)) for i in span
        ]
        rows = [jnp.broadcast_to(work[first + i : first + i + 1, :], (8, width)) for i in span]
        small = {}
        for i in span:
            for j in range(i, GROUP):
                small[i, j] = jnp.broadcast_to(cols[i][first + j : first + j + 1, :], (8, width))
        ratio = {}
        recip = []
        for i in span:
            recip.append(1.0 / small[i, i])
            for j in range(i + 1, GROUP):
                ratio[i, j] = small[i, j] * recip[i]
            for j in range(i + 1, GROUP):
                for k in range(j, GROUP):
                    small[j, k] = small[j, k] - ratio[i, j] * small[i, k]
        update = None
        for i in span:
            scaled = jnp.where(row > first + i, cols[i] * tall(recip[i]), 0.0)
            pivots = jnp.where(row == first + i, tall(small[i, i]), pivots)
            for j in range(i + 1, GROUP):
                cols[j] = cols[j] - cols[i] * tall(ratio[i, j])
                rows[j] = rows[j] - ratio[i, j] * rows[i]
            term = scaled * tall(rows[i])
            update = term if update is None else update + term
        work = work - update
    return work[:, step:width] * lax.rsqrt(pivots)[:, :step]


def invert(corner, out_ref, work_ref):
    size = corner.shape[0]
    step = STEP
    row = lax.broadcasted_iota(jnp.int32, (size, size), 0)
    col = lax.broadcasted_iota(jnp.int32, (size, size), 1)
    work_ref[:, :size] = corner
    work_ref[:, size:] = (row == col).astype(jnp.float32)
    small_row = lax.broadcasted_iota(jnp.int32, (step, step), 0)
    small_col = lax.broadcasted_iota(jnp.int32, (step, step), 1)
    eye = (small_row == small_col).astype(jnp.float32)
    for start in range(0, size, step):
        stop = start + step
        lead = eliminate(work_ref[start:stop, start:stop], eye, step)
        upper = matmul(lead, work_ref[start:stop, :])
        out_ref[start:stop, :] = upper[:, size:]
        if stop < size:
            work_ref[stop:, :] = work_ref[stop:, :] - matmul_tn(upper[:, stop:size], upper)


def inverse_kernel(corner_ref, out_ref, work_ref):
    invert(corner_ref[...], out_ref, work_ref)


def lower_inverse(corner):
    size = corner.shape[0]
    return pl.pallas_call(
        inverse_kernel,
        out_shape=jax.ShapeDtypeStruct((size, size), jnp.float32),
        scratch_shapes=[pltpu.VMEM((size, 2 * size), jnp.float32)],
        name="lower_inverse",
    )(corner)


def parent_kernel(where_ref, inverse_ref, tops_ref, top_ref, parent_ref, out_ref):
    row_id, own_column = where_ref[0], where_ref[1]
    lead = PANEL // BLOCK
    blocks = tops_ref.shape[0]

    @pl.when(own_column >= lead)
    def _():
        upper = matmul(inverse_ref[...], top_ref[...])

        def body(block, carry):
            part = pl.ds(pl.multiple_of(block * BLOCK, BLOCK), BLOCK)
            change = matmul_tn(matmul(inverse_ref[...], tops_ref[block]), upper)
            first = (row_id == 0) & (block < lead)
            out_ref[part, :] = parent_ref[part, :] - jnp.where(first, 0.0, change)
            return carry

        lax.fori_loop(0, blocks, body, 0)

    @pl.when(own_column < lead)
    def _():
        start = pl.multiple_of(jnp.minimum(own_column, lead - 1) * BLOCK, BLOCK)
        rows = inverse_ref[pl.ds(start, BLOCK), :]

        def body(block, carry):
            part = pl.ds(pl.multiple_of(block * BLOCK, BLOCK), BLOCK)
            out_ref[part, :] = matmul(rows, tops_ref[block]).T
            return carry

        lax.fori_loop(0, blocks, body, 0)


def parent_base(where, inverse, tops, top, parent):
    vmem = pl.BlockSpec(memory_space=pltpu.VMEM)
    return pl.pallas_call(
        parent_kernel,
        out_shape=jax.ShapeDtypeStruct(parent.shape, jnp.float32),
        in_specs=[pl.BlockSpec(memory_space=pltpu.SMEM), vmem, vmem, vmem, vmem],
        out_specs=vmem,
        name="parent_base",
    )(where, inverse, tops, top, parent)


def pick_kernel(index_ref, front_ref, out_ref):
    out_ref[0] = front_ref[...]


def pick_columns(index, front):
    rows = front.shape[0]
    count = index.shape[0]
    return pl.pallas_call(
        pick_kernel,
        out_shape=jax.ShapeDtypeStruct((count, rows, BLOCK), jnp.float32),
        grid_spec=pltpu.PrefetchScalarGridSpec(
            num_scalar_prefetch=1,
            grid=(count,),
            in_specs=[pl.BlockSpec((rows, BLOCK), lambda i, index: (0, index[i]))],
            out_specs=pl.BlockSpec((1, rows, BLOCK), lambda i, index: (i, 0, 0)),
        ),
        name="pick_columns",
    )(index, front)


def schur_kernel(
    slot_ref, live_ref, piece_ref, valid_ref, cols_ref, factor_ref, inverse_ref, block_ref,
    out_ref, top_ref, tmp_ref, sems, top_sems,
):
    leaves = live_ref.shape[0]
    bands = valid_ref.shape[0]

    def copies(leaf, dest):
        start = pl.multiple_of(piece_ref[dest] * BLOCK, BLOCK)
        piece = tmp_ref.at[leaf, pl.ds(start, BLOCK), :]
        item = leaf * bands + dest
        yield pltpu.make_async_copy(piece, out_ref.at[item], sems.at[item])
        if dest == 0:
            yield pltpu.make_async_copy(piece, top_ref.at[leaf], top_sems.at[leaf])

    def each(leaf, act):
        for dest in range(bands):

            @pl.when(valid_ref[dest] > 0)
            def _(dest=dest):
                for copy in copies(leaf, dest):
                    act(copy)

    def start(leaf, carry):
        @pl.when(live_ref[leaf] > 0)
        def _():
            slot = slot_ref[leaf]
            block = matmul_nt(block_ref[slot], inverse_ref[...])
            tmp_ref[leaf] = cols_ref[slot] - matmul_nt(factor_ref[...], block)
            each(leaf, lambda copy: copy.start())

        return carry

    def finish(leaf, carry):
        @pl.when(live_ref[leaf] > 0)
        def _():
            each(leaf, lambda copy: copy.wait())

        return carry

    lax.fori_loop(0, leaves, start, 0)
    lax.fori_loop(0, leaves, finish, 0)


def schur_pieces(slot, live, piece, valid, cols, factor, inverse, blocks):
    leaves = slot.shape[0]
    bands = piece.shape[0]
    rows = factor.shape[0]
    smem = pl.BlockSpec(memory_space=pltpu.SMEM)
    vmem = pl.BlockSpec(memory_space=pltpu.VMEM)
    anywhere = pl.BlockSpec(memory_space=pl.ANY)
    return pl.pallas_call(
        schur_kernel,
        out_shape=(
            jax.ShapeDtypeStruct((leaves * bands, BLOCK, BLOCK), jnp.float32),
            jax.ShapeDtypeStruct((leaves, BLOCK, BLOCK), jnp.float32),
        ),
        in_specs=[smem] * 4 + [vmem] * 4,
        out_specs=(anywhere, anywhere),
        scratch_shapes=[
            pltpu.VMEM((leaves, rows, BLOCK), jnp.float32),
            pltpu.SemaphoreType.DMA((leaves * bands,)),
            pltpu.SemaphoreType.DMA((leaves,)),
        ],
        name="schur_pieces",
    )(slot, live, piece, valid, cols, factor, inverse, blocks)


def place_kernel(slot_ref, base_ref, blocks_ref, out_ref):
    out_ref[...] = base_ref[...]

    def body(item, carry):
        slot = slot_ref[item]

        @pl.when(slot >= 0)
        def _():
            start = pl.multiple_of(slot * BLOCK, BLOCK)
            out_ref[pl.ds(start, BLOCK), :] += blocks_ref[item]

        return carry

    lax.fori_loop(0, blocks_ref.shape[0], body, 0)


def place_blocks(slots, base, blocks):
    vmem = pl.BlockSpec(memory_space=pltpu.VMEM)
    return pl.pallas_call(
        place_kernel,
        out_shape=jax.ShapeDtypeStruct(base.shape, jnp.float32),
        in_specs=[pl.BlockSpec(memory_space=pltpu.SMEM), vmem, vmem],
        out_specs=vmem,
        name="place_blocks",
    )(slots, base, blocks)


def locate(values, usable, count):
    hit = (values[..., None, :] == jnp.arange(count)[:, None]) & usable[..., None, :]
    index = jnp.sum(jnp.where(hit, jnp.arange(values.shape[-1]), 0), axis=-1)
    return index.astype(jnp.int32), jnp.any(hit, axis=-1)


def at(value, index, axis=0):
    return lax.dynamic_index_in_dim(value, index, axis, keepdims=False)


def swapped_core(along):
    other = lax.ppermute(along, "col_1", [(0, 1), (1, 0)])
    first = lax.axis_index("col_1") == 0
    both = jnp.stack([jnp.where(first, along, other), jnp.where(first, other, along)], axis=1)
    return both.reshape(-1, *along.shape[1:])


def from_first(value, axis, stride=None):
    index = lax.axis_index(axis)
    stride = stride or lax.axis_size(axis) // 2
    while stride:
        value = tree_round(value, axis, index, stride)
        stride //= 2
    return value


def tree_round(value, axis, index, stride):
    pairs = [(i, i + stride) for i in range(0, lax.axis_size(axis), 2 * stride)]
    other = lax.ppermute(value, axis, pairs)
    return jnp.where(index % (2 * stride) == stride, other, value)


def per_device(child_front, parent_front, block_map):
    front = child_front[0]
    parent = parent_front[:, 0, 0, :]
    grid_rows = lax.axis_size("row")
    grid_cols = lax.axis_size(COL)
    leaves = lax.axis_size("leaf")
    row_id = lax.axis_index("row")
    col_id = lax.axis_index(COL)
    leaf_id = lax.axis_index("leaf")
    rows = front.shape[0]
    child_blocks = rows // BLOCK
    lead = PANEL // BLOCK
    parent_rows = parent.shape[0]

    padded = jnp.concatenate([jnp.full((leaves, lead), -1, jnp.int32), block_map], axis=1)
    maps = padded.reshape(leaves, grid_rows, child_blocks)
    usable = maps >= 0
    band = maps // grid_cols
    residue = maps % grid_cols
    lo_index, lo_valid = locate(residue, usable, grid_cols)
    hi_index, hi_valid = locate(band, usable, grid_rows)
    own_lo_index, own_lo_valid = at(lo_index, leaf_id), at(lo_valid, leaf_id)
    column_index = at(own_lo_index, col_id, 1)
    column_valid = at(own_lo_valid, col_id, 1)

    share = PANEL // grid_cols
    deals = front[:, :PANEL].reshape(-1, grid_cols, share, PANEL).transpose(1, 0, 2, 3)
    deal = exchange(deals.reshape(grid_cols, -1, PANEL), COL)[0]
    picked = pick_columns(at(own_lo_index, col_id), front)
    deal, picked = lax.optimization_barrier((deal, picked))
    along = spread(deal, "col_0", lax.axis_size("col_0"))
    half = grid_rows // 2
    corner = tree_round(deal[:share], "row", row_id, half)
    parent_top = from_first(parent[:PANEL], "row")
    corner, along = lax.optimization_barrier((corner, along))
    raw = swapped_core(along).reshape(grid_cols, -1, share, PANEL)
    raw = raw.transpose(1, 0, 2, 3).reshape(rows, PANEL)
    mine = lax.dynamic_slice_in_dim(raw, at(column_index, row_id) * BLOCK, BLOCK, 0)
    corner, mine = lax.optimization_barrier((from_first(corner, "row", half // 2), mine))
    blocks = lax.all_gather(mine, "row")
    corner = spread(corner, "col_0", lax.axis_size("col_0"))
    picked, corner, parent_top = lax.optimization_barrier((picked, corner, parent_top))
    corner = swapped_core(corner).reshape(PANEL, PANEL)
    cols = exchange(picked, COL)
    inverse = lower_inverse(corner)
    factor = matmul_nt(raw, inverse)

    column_band = jnp.sum(
        jnp.where(jnp.arange(child_blocks) == column_index[:, None], at(band, leaf_id), 0), axis=-1
    )
    slot, slot_valid = locate(column_band, column_valid, leaves)
    pieces, tops = schur_pieces(
        slot,
        slot_valid.astype(jnp.int32),
        at(at(hi_index, leaf_id), row_id),
        at(at(hi_valid, leaf_id), row_id).astype(jnp.int32),
        cols,
        factor,
        inverse,
        blocks,
    )

    own_column = leaf_id * grid_cols + col_id
    present = jnp.any((maps == own_column) & usable, axis=(1, 2))
    row_slot = jnp.sum(
        jnp.where(jnp.arange(child_blocks) == hi_index[..., None], residue[:, :, None, :], 0),
        axis=-1,
    )
    row_slot = jnp.where(hi_valid & present[:, None, None], row_slot, -1).astype(jnp.int32)

    tops = exchange(tops.reshape(leaves * grid_rows, -1, BLOCK), LEAF_ROW)
    chosen = row_slot[:, :, 0].reshape(-1) == jnp.arange(lead)[:, None]
    top = jnp.sum(jnp.where(chosen[:, :, None, None], tops, 0.0), axis=1)
    top = spread(top, "row", grid_rows).transpose(1, 0, 2, 3).reshape(PANEL, BLOCK) + parent_top
    arrived = exchange(pieces, LEAF_ROW)

    every_leaf = lax.all_gather(top, "leaf")
    tops = lax.all_gather(at(every_leaf, row_id), COL)
    corner = from_first(every_leaf[0], "col_0")
    corner = lower_inverse(jnp.concatenate(list(swapped_core(corner[None])), axis=1))
    place = jnp.stack([row_id, own_column]).astype(jnp.int32)
    base = parent_base(place, corner, tops, top, parent)
    slots = jnp.where(own_column < lead, -1, at(row_slot, row_id, 2)).reshape(-1)
    result = place_blocks(slots, base, arrived)
    return (factor[None], result[:, None, None, :])


def solution(mesh):
    torus = Mesh(
        mesh.devices.reshape(mesh.shape["leaf"], mesh.shape["row"], 4, 2),
        ("leaf", "row", "col_0", "col_1"),
    )
    in_specs = (P("leaf", "row", COL), P("row", None, LEAF_COL, None), P())
    out_specs = (P("leaf", "row", None), P("row", None, LEAF_COL, None))
    return jax.shard_map(
        per_device, mesh=torus, in_specs=in_specs, out_specs=out_specs, check_vma=False
    )
```

```python
import jax
import jax.numpy as jnp
from jax import lax
from jax.experimental import pallas as pl
from jax.experimental.pallas import tpu as pltpu
from jax.sharding import Mesh
from jax.sharding import PartitionSpec as P

FP = 8192
PANEL = 256
BLOCK = 128
COL = ("col_0", "col_1")
LEAF_COL = ("leaf", "col_0", "col_1")
LEAF_ROW = ("leaf", "row")
HIGHEST = lax.Precision.HIGHEST
STEP = 64
GROUP = 8


def matmul(left, right):
    return jnp.dot(left, right, precision=HIGHEST, preferred_element_type=jnp.float32)


def matmul_nt(left, right):
    return lax.dot_general(
        left,
        right,
        (((1,), (1,)), ((), ())),
        precision=HIGHEST,
        preferred_element_type=jnp.float32,
    )


def matmul_tn(left, right):
    return lax.dot_general(
        left,
        right,
        (((0,), (0,)), ((), ())),
        precision=HIGHEST,
        preferred_element_type=jnp.float32,
    )


def exchange(value, axes):
    return lax.all_to_all(value, axes, split_axis=0, concat_axis=0, tiled=True)


def spread(value, axes, count):
    return exchange(jnp.broadcast_to(value[None], (count, *value.shape)), axes)


def eliminate(tile, eye, step):
    width = 2 * step
    row = lax.broadcasted_iota(jnp.int32, (step, width), 0)
    work = jnp.concatenate([tile, eye], axis=1)
    pivots = jnp.ones((step, width), jnp.float32)

    def tall(value):
        return jnp.concatenate([value] * (step // 8), axis=0)

    for first in range(0, step, GROUP):
        span = range(GROUP)
        cols = [
            jnp.broadcast_to(work[:, first + i : first + i + 1], (step, width)) for i in span
        ]
        rows = [jnp.broadcast_to(work[first + i : first + i + 1, :], (8, width)) for i in span]
        small = {}
        for i in span:
            for j in range(i, GROUP):
                small[i, j] = jnp.broadcast_to(cols[i][first + j : first + j + 1, :], (8, width))
        ratio = {}
        recip = []
        for i in span:
            recip.append(1.0 / small[i, i])
            for j in range(i + 1, GROUP):
                ratio[i, j] = small[i, j] * recip[i]
            for j in range(i + 1, GROUP):
                for k in range(j, GROUP):
                    small[j, k] = small[j, k] - ratio[i, j] * small[i, k]
        update = None
        for i in span:
            scaled = jnp.where(row > first + i, cols[i] * tall(recip[i]), 0.0)
            pivots = jnp.where(row == first + i, tall(small[i, i]), pivots)
            for j in range(i + 1, GROUP):
                cols[j] = cols[j] - cols[i] * tall(ratio[i, j])
                rows[j] = rows[j] - ratio[i, j] * rows[i]
            term = scaled * tall(rows[i])
            update = term if update is None else update + term
        work = work - update
    return work[:, step:width] * lax.rsqrt(pivots)[:, :step]


def invert(corner, out_ref, work_ref):
    size = corner.shape[0]
    step = STEP
    row = lax.broadcasted_iota(jnp.int32, (size, size), 0)
    col = lax.broadcasted_iota(jnp.int32, (size, size), 1)
    work_ref[:, :size] = corner
    work_ref[:, size:] = (row == col).astype(jnp.float32)
    small_row = lax.broadcasted_iota(jnp.int32, (step, step), 0)
    small_col = lax.broadcasted_iota(jnp.int32, (step, step), 1)
    eye = (small_row == small_col).astype(jnp.float32)
    for start in range(0, size, step):
        stop = start + step
        lead = eliminate(work_ref[start:stop, start:stop], eye, step)
        upper = matmul(lead, work_ref[start:stop, :])
        out_ref[start:stop, :] = upper[:, size:]
        if stop < size:
            work_ref[stop:, :] = work_ref[stop:, :] - matmul_tn(upper[:, stop:size], upper)


def inverse_kernel(corner_ref, out_ref, work_ref):
    invert(corner_ref[...], out_ref, work_ref)


def lower_inverse(corner):
    size = corner.shape[0]
    return pl.pallas_call(
        inverse_kernel,
        out_shape=jax.ShapeDtypeStruct((size, size), jnp.float32),
        scratch_shapes=[pltpu.VMEM((size, 2 * size), jnp.float32)],
        name="lower_inverse",
    )(corner)


def parent_kernel(where_ref, inverse_ref, tops_ref, top_ref, parent_ref, out_ref):
    row_id, own_column = where_ref[0], where_ref[1]
    lead = PANEL // BLOCK
    blocks = tops_ref.shape[0]

    @pl.when(own_column >= lead)
    def _():
        upper = matmul(inverse_ref[...], top_ref[...])

        def body(block, carry):
            part = pl.ds(pl.multiple_of(block * BLOCK, BLOCK), BLOCK)
            change = matmul_tn(matmul(inverse_ref[...], tops_ref[block]), upper)
            first = (row_id == 0) & (block < lead)
            out_ref[part, :] = parent_ref[part, :] - jnp.where(first, 0.0, change)
            return carry

        lax.fori_loop(0, blocks, body, 0)

    @pl.when(own_column < lead)
    def _():
        start = pl.multiple_of(jnp.minimum(own_column, lead - 1) * BLOCK, BLOCK)
        rows = inverse_ref[pl.ds(start, BLOCK), :]

        def body(block, carry):
            part = pl.ds(pl.multiple_of(block * BLOCK, BLOCK), BLOCK)
            out_ref[part, :] = matmul(rows, tops_ref[block]).T
            return carry

        lax.fori_loop(0, blocks, body, 0)


def parent_base(where, inverse, tops, top, parent):
    vmem = pl.BlockSpec(memory_space=pltpu.VMEM)
    return pl.pallas_call(
        parent_kernel,
        out_shape=jax.ShapeDtypeStruct(parent.shape, jnp.float32),
        in_specs=[pl.BlockSpec(memory_space=pltpu.SMEM), vmem, vmem, vmem, vmem],
        out_specs=vmem,
        name="parent_base",
    )(where, inverse, tops, top, parent)


def pick_kernel(index_ref, front_ref, out_ref):
    out_ref[0] = front_ref[...]


def pick_columns(index, front):
    rows = front.shape[0]
    count = index.shape[0]
    return pl.pallas_call(
        pick_kernel,
        out_shape=jax.ShapeDtypeStruct((count, rows, BLOCK), jnp.float32),
        grid_spec=pltpu.PrefetchScalarGridSpec(
            num_scalar_prefetch=1,
            grid=(count,),
            in_specs=[pl.BlockSpec((rows, BLOCK), lambda i, index: (0, index[i]))],
            out_specs=pl.BlockSpec((1, rows, BLOCK), lambda i, index: (i, 0, 0)),
        ),
        name="pick_columns",
    )(index, front)


def schur_kernel(
    slot_ref, live_ref, piece_ref, valid_ref, cols_ref, factor_ref, inverse_ref, block_ref,
    out_ref, top_ref, tmp_ref, sems, top_sems,
):
    leaves = live_ref.shape[0]
    bands = valid_ref.shape[0]

    def copies(leaf, dest):
        start = pl.multiple_of(piece_ref[dest] * BLOCK, BLOCK)
        piece = tmp_ref.at[leaf, pl.ds(start, BLOCK), :]
        item = leaf * bands + dest
        yield pltpu.make_async_copy(piece, out_ref.at[item], sems.at[item])
        if dest == 0:
            yield pltpu.make_async_copy(piece, top_ref.at[leaf], top_sems.at[leaf])

    def each(leaf, act):
        for dest in range(bands):

            @pl.when(valid_ref[dest] > 0)
            def _(dest=dest):
                for copy in copies(leaf, dest):
                    act(copy)

    def start(leaf, carry):
        @pl.when(live_ref[leaf] > 0)
        def _():
            slot = slot_ref[leaf]
            block = matmul_nt(block_ref[slot], inverse_ref[...])
            tmp_ref[leaf] = cols_ref[slot] - matmul_nt(factor_ref[...], block)
            each(leaf, lambda copy: copy.start())

        return carry

    def finish(leaf, carry):
        @pl.when(live_ref[leaf] > 0)
        def _():
            each(leaf, lambda copy: copy.wait())

        return carry

    lax.fori_loop(0, leaves, start, 0)
    lax.fori_loop(0, leaves, finish, 0)


def schur_pieces(slot, live, piece, valid, cols, factor, inverse, blocks):
    leaves = slot.shape[0]
    bands = piece.shape[0]
    rows = factor.shape[0]
    smem = pl.BlockSpec(memory_space=pltpu.SMEM)
    vmem = pl.BlockSpec(memory_space=pltpu.VMEM)
    anywhere = pl.BlockSpec(memory_space=pl.ANY)
    return pl.pallas_call(
        schur_kernel,
        out_shape=(
            jax.ShapeDtypeStruct((leaves * bands, BLOCK, BLOCK), jnp.float32),
            jax.ShapeDtypeStruct((leaves, BLOCK, BLOCK), jnp.float32),
        ),
        in_specs=[smem] * 4 + [vmem] * 4,
        out_specs=(anywhere, anywhere),
        scratch_shapes=[
            pltpu.VMEM((leaves, rows, BLOCK), jnp.float32),
            pltpu.SemaphoreType.DMA((leaves * bands,)),
            pltpu.SemaphoreType.DMA((leaves,)),
        ],
        name="schur_pieces",
    )(slot, live, piece, valid, cols, factor, inverse, blocks)


def place_kernel(slot_ref, base_ref, blocks_ref, out_ref):
    out_ref[...] = base_ref[...]

    def body(item, carry):
        slot = slot_ref[item]

        @pl.when(slot >= 0)
        def _():
            start = pl.multiple_of(slot * BLOCK, BLOCK)
            out_ref[pl.ds(start, BLOCK), :] += blocks_ref[item]

        return carry

    lax.fori_loop(0, blocks_ref.shape[0], body, 0)


def place_blocks(slots, base, blocks):
    vmem = pl.BlockSpec(memory_space=pltpu.VMEM)
    return pl.pallas_call(
        place_kernel,
        out_shape=jax.ShapeDtypeStruct(base.shape, jnp.float32),
        in_specs=[pl.BlockSpec(memory_space=pltpu.SMEM), vmem, vmem],
        out_specs=vmem,
        name="place_blocks",
    )(slots, base, blocks)


def locate(values, usable, count):
    hit = (values[..., None, :] == jnp.arange(count)[:, None]) & usable[..., None, :]
    index = jnp.sum(jnp.where(hit, jnp.arange(values.shape[-1]), 0), axis=-1)
    return index.astype(jnp.int32), jnp.any(hit, axis=-1)


def at(value, index, axis=0):
    return lax.dynamic_index_in_dim(value, index, axis, keepdims=False)


def swapped_core(along):
    other = lax.ppermute(along, "col_1", [(0, 1), (1, 0)])
    first = lax.axis_index("col_1") == 0
    both = jnp.stack([jnp.where(first, along, other), jnp.where(first, other, along)], axis=1)
    return both.reshape(-1, *along.shape[1:])


def from_first(value, axis, stride=None):
    index = lax.axis_index(axis)
    stride = stride or lax.axis_size(axis) // 2
    while stride:
        value = tree_round(value, axis, index, stride)
        stride //= 2
    return value


def tree_round(value, axis, index, stride):
    pairs = [(i, i + stride) for i in range(0, lax.axis_size(axis), 2 * stride)]
    other = lax.ppermute(value, axis, pairs)
    return jnp.where(index % (2 * stride) == stride, other, value)


def per_device(child_front, parent_front, block_map):
    front = child_front[0]
    parent = parent_front[:, 0, 0, :]
    grid_rows = lax.axis_size("row")
    grid_cols = lax.axis_size(COL)
    leaves = lax.axis_size("leaf")
    row_id = lax.axis_index("row")
    col_id = lax.axis_index(COL)
    leaf_id = lax.axis_index("leaf")
    rows = front.shape[0]
    child_blocks = rows // BLOCK
    lead = PANEL // BLOCK
    parent_rows = parent.shape[0]

    padded = jnp.concatenate([jnp.full((leaves, lead), -1, jnp.int32), block_map], axis=1)
    maps = padded.reshape(leaves, grid_rows, child_blocks)
    usable = maps >= 0
    band = maps // grid_cols
    residue = maps % grid_cols
    lo_index, lo_valid = locate(residue, usable, grid_cols)
    hi_index, hi_valid = locate(band, usable, grid_rows)
    own_lo_index, own_lo_valid = at(lo_index, leaf_id), at(lo_valid, leaf_id)
    column_index = at(own_lo_index, col_id, 1)
    column_valid = at(own_lo_valid, col_id, 1)

    half = grid_rows // 2
    deal = exchange(front[:, :PANEL].reshape(grid_cols, -1, PANEL), COL)[0]
    picked = pick_columns(at(own_lo_index, col_id), front)
    parent_top = tree_round(parent[:PANEL], "row", row_id, half)
    deal, picked, parent_top = lax.optimization_barrier((deal, picked, parent_top))
    along = spread(deal, "col_0", lax.axis_size("col_0"))
    parent_top = tree_round(parent_top, "row", row_id, half // 2)
    along, parent_top = lax.optimization_barrier((along, parent_top))
    raw = swapped_core(along)
    parent_top = from_first(parent_top, "row", half // 4)
    picked, raw, parent_top = lax.optimization_barrier((picked, raw, parent_top))
    cols = exchange(picked, COL)
    raw = raw.reshape(rows, PANEL)
    mine = lax.dynamic_slice_in_dim(raw, at(column_index, row_id) * BLOCK, BLOCK, 0)
    blocks = lax.all_gather(mine, "row")
    inverse = lower_inverse(from_first(raw[:PANEL], "row"))
    factor = matmul_nt(raw, inverse)

    column_band = jnp.sum(
        jnp.where(jnp.arange(child_blocks) == column_index[:, None], at(band, leaf_id), 0), axis=-1
    )
    slot, slot_valid = locate(column_band, column_valid, leaves)
    pieces, tops = schur_pieces(
        slot,
        slot_valid.astype(jnp.int32),
        at(at(hi_index, leaf_id), row_id),
        at(at(hi_valid, leaf_id), row_id).astype(jnp.int32),
        cols,
        factor,
        inverse,
        blocks,
    )

    own_column = leaf_id * grid_cols + col_id
    present = jnp.any((maps == own_column) & usable, axis=(1, 2))
    row_slot = jnp.sum(
        jnp.where(jnp.arange(child_blocks) == hi_index[..., None], residue[:, :, None, :], 0),
        axis=-1,
    )
    row_slot = jnp.where(hi_valid & present[:, None, None], row_slot, -1).astype(jnp.int32)

    tops = exchange(tops.reshape(leaves * grid_rows, -1, BLOCK), LEAF_ROW)
    chosen = row_slot[:, :, 0].reshape(-1) == jnp.arange(lead)[:, None]
    top = jnp.sum(jnp.where(chosen[:, :, None, None], tops, 0.0), axis=1)
    top = spread(top, "row", grid_rows).transpose(1, 0, 2, 3).reshape(PANEL, BLOCK) + parent_top
    arrived = exchange(pieces, LEAF_ROW)

    every_leaf = lax.all_gather(top, "leaf")
    tops = lax.all_gather(at(every_leaf, row_id), COL)
    corner = from_first(every_leaf[0], "col_0")
    corner = lower_inverse(jnp.concatenate(list(swapped_core(corner[None])), axis=1))
    place = jnp.stack([row_id, own_column]).astype(jnp.int32)
    base = parent_base(place, corner, tops, top, parent)
    slots = jnp.where(own_column < lead, -1, at(row_slot, row_id, 2)).reshape(-1)
    result = place_blocks(slots, base, arrived)
    return (factor[None], result[:, None, None, :])


def solution(mesh):
    torus = Mesh(
        mesh.devices.reshape(mesh.shape["leaf"], mesh.shape["row"], 4, 2),
        ("leaf", "row", "col_0", "col_1"),
    )
    in_specs = (P("leaf", "row", COL), P("row", None, LEAF_COL, None), P())
    out_specs = (P("leaf", "row", None), P("row", None, LEAF_COL, None))
    return jax.shard_map(
        per_device, mesh=torus, in_specs=in_specs, out_specs=out_specs, check_vma=False
    )
```

```python
import jax
import jax.numpy as jnp
from jax import lax
from jax.experimental import pallas as pl
from jax.experimental.pallas import tpu as pltpu
from jax.sharding import Mesh
from jax.sharding import PartitionSpec as P

PANEL = 256
BLOCK = 128
COL = ("col_0", "col_1")
LEAF_COL = ("leaf", "col_0", "col_1")
LEAF_ROW = ("leaf", "row")
HIGHEST = lax.Precision.HIGHEST
STEP = 64
GROUP = 8


def matmul(left, right):
    return jnp.dot(left, right, precision=HIGHEST, preferred_element_type=jnp.float32)


def matmul_nt(left, right):
    return lax.dot_general(
        left,
        right,
        (((1,), (1,)), ((), ())),
        precision=HIGHEST,
        preferred_element_type=jnp.float32,
    )


def matmul_tn(left, right):
    return lax.dot_general(
        left,
        right,
        (((0,), (0,)), ((), ())),
        precision=HIGHEST,
        preferred_element_type=jnp.float32,
    )


def exchange(value, axes):
    return lax.all_to_all(value, axes, split_axis=0, concat_axis=0, tiled=True)


def spread(value, axes, count):
    return exchange(jnp.broadcast_to(value[None], (count, *value.shape)), axes)


def eliminate(tile, eye, step):
    width = 2 * step
    row = lax.broadcasted_iota(jnp.int32, (step, width), 0)
    work = jnp.concatenate([tile, eye], axis=1)
    pivots = jnp.ones((step, width), jnp.float32)

    def tall(value):
        return jnp.concatenate([value] * (step // 8), axis=0)

    for first in range(0, step, GROUP):
        span = range(GROUP)
        cols = [
            jnp.broadcast_to(work[:, first + i : first + i + 1], (step, width)) for i in span
        ]
        rows = [jnp.broadcast_to(work[first + i : first + i + 1, :], (8, width)) for i in span]
        small = {}
        for i in span:
            for j in range(i, GROUP):
                small[i, j] = jnp.broadcast_to(cols[i][first + j : first + j + 1, :], (8, width))
        ratio = {}
        recip = []
        for i in span:
            recip.append(1.0 / small[i, i])
            for j in range(i + 1, GROUP):
                ratio[i, j] = small[i, j] * recip[i]
            for j in range(i + 1, GROUP):
                for k in range(j, GROUP):
                    small[j, k] = small[j, k] - ratio[i, j] * small[i, k]
        update = None
        for i in span:
            scaled = jnp.where(row > first + i, cols[i] * tall(recip[i]), 0.0)
            pivots = jnp.where(row == first + i, tall(small[i, i]), pivots)
            for j in range(i + 1, GROUP):
                cols[j] = cols[j] - cols[i] * tall(ratio[i, j])
                rows[j] = rows[j] - ratio[i, j] * rows[i]
            term = scaled * tall(rows[i])
            update = term if update is None else update + term
        work = work - update
    return work[:, step:width] * lax.rsqrt(pivots)[:, :step]


def invert(corner, out_ref, work_ref):
    size = corner.shape[0]
    step = STEP
    row = lax.broadcasted_iota(jnp.int32, (size, size), 0)
    col = lax.broadcasted_iota(jnp.int32, (size, size), 1)
    work_ref[:, :size] = corner
    work_ref[:, size:] = (row == col).astype(jnp.float32)
    small_row = lax.broadcasted_iota(jnp.int32, (step, step), 0)
    small_col = lax.broadcasted_iota(jnp.int32, (step, step), 1)
    eye = (small_row == small_col).astype(jnp.float32)
    for start in range(0, size, step):
        stop = start + step
        lead = eliminate(work_ref[start:stop, start:stop], eye, step)
        upper = matmul(lead, work_ref[start:stop, :])
        out_ref[start:stop, :] = upper[:, size:]
        if stop < size:
            work_ref[stop:, :] = work_ref[stop:, :] - matmul_tn(upper[:, stop:size], upper)


def inverse_kernel(corner_ref, out_ref, work_ref):
    invert(corner_ref[...], out_ref, work_ref)


def lower_inverse(corner):
    size = corner.shape[0]
    return pl.pallas_call(
        inverse_kernel,
        out_shape=jax.ShapeDtypeStruct((size, size), jnp.float32),
        scratch_shapes=[pltpu.VMEM((size, 2 * size), jnp.float32)],
        name="lower_inverse",
    )(corner)


def parent_kernel(where_ref, inverse_ref, tops_ref, top_ref, parent_ref, out_ref):
    row_id, own_column = where_ref[0], where_ref[1]
    lead = PANEL // BLOCK
    blocks = tops_ref.shape[0]

    @pl.when(own_column >= lead)
    def _():
        upper = matmul(inverse_ref[...], top_ref[...])

        def body(block, carry):
            part = pl.ds(pl.multiple_of(block * BLOCK, BLOCK), BLOCK)
            change = matmul_tn(matmul(inverse_ref[...], tops_ref[block]), upper)
            first = (row_id == 0) & (block < lead)
            out_ref[part, :] = parent_ref[part, :] - jnp.where(first, 0.0, change)
            return carry

        lax.fori_loop(0, blocks, body, 0)

    @pl.when(own_column < lead)
    def _():
        start = pl.multiple_of(jnp.minimum(own_column, lead - 1) * BLOCK, BLOCK)
        rows = inverse_ref[pl.ds(start, BLOCK), :]

        def body(block, carry):
            part = pl.ds(pl.multiple_of(block * BLOCK, BLOCK), BLOCK)
            out_ref[part, :] = matmul(rows, tops_ref[block]).T
            return carry

        lax.fori_loop(0, blocks, body, 0)


def parent_base(where, inverse, tops, top, parent):
    vmem = pl.BlockSpec(memory_space=pltpu.VMEM)
    return pl.pallas_call(
        parent_kernel,
        out_shape=jax.ShapeDtypeStruct(parent.shape, jnp.float32),
        in_specs=[pl.BlockSpec(memory_space=pltpu.SMEM), vmem, vmem, vmem, vmem],
        out_specs=vmem,
        name="parent_base",
    )(where, inverse, tops, top, parent)


def pick_kernel(index_ref, front_ref, out_ref):
    out_ref[0] = front_ref[...]


def pick_columns(index, front):
    rows = front.shape[0]
    count = index.shape[0]
    return pl.pallas_call(
        pick_kernel,
        out_shape=jax.ShapeDtypeStruct((count, rows, BLOCK), jnp.float32),
        grid_spec=pltpu.PrefetchScalarGridSpec(
            num_scalar_prefetch=1,
            grid=(count,),
            in_specs=[pl.BlockSpec((rows, BLOCK), lambda i, index: (0, index[i]))],
            out_specs=pl.BlockSpec((1, rows, BLOCK), lambda i, index: (i, 0, 0)),
        ),
        name="pick_columns",
    )(index, front)


def schur_kernel(
    slot_ref, live_ref, piece_ref, valid_ref, cols_ref, factor_ref, inverse_ref, block_ref,
    out_ref, top_ref, tmp_ref, sems, top_sems,
):
    leaves = live_ref.shape[0]
    bands = valid_ref.shape[0]

    def copies(leaf, dest):
        start = pl.multiple_of(piece_ref[dest] * BLOCK, BLOCK)
        piece = tmp_ref.at[leaf, pl.ds(start, BLOCK), :]
        item = leaf * bands + dest
        yield pltpu.make_async_copy(piece, out_ref.at[item], sems.at[item])
        if dest == 0:
            yield pltpu.make_async_copy(piece, top_ref.at[leaf], top_sems.at[leaf])

    def each(leaf, act):
        for dest in range(bands):

            @pl.when(valid_ref[dest] > 0)
            def _(dest=dest):
                for copy in copies(leaf, dest):
                    act(copy)

    def start(leaf, carry):
        @pl.when(live_ref[leaf] > 0)
        def _():
            slot = slot_ref[leaf]
            block = matmul_nt(block_ref[slot], inverse_ref[...])
            tmp_ref[leaf] = cols_ref[slot] - matmul_nt(factor_ref[...], block)
            each(leaf, lambda copy: copy.start())

        return carry

    def finish(leaf, carry):
        @pl.when(live_ref[leaf] > 0)
        def _():
            each(leaf, lambda copy: copy.wait())

        return carry

    lax.fori_loop(0, leaves, start, 0)
    lax.fori_loop(0, leaves, finish, 0)


def schur_pieces(slot, live, piece, valid, cols, factor, inverse, blocks):
    leaves = slot.shape[0]
    bands = piece.shape[0]
    rows = factor.shape[0]
    smem = pl.BlockSpec(memory_space=pltpu.SMEM)
    vmem = pl.BlockSpec(memory_space=pltpu.VMEM)
    anywhere = pl.BlockSpec(memory_space=pl.ANY)
    return pl.pallas_call(
        schur_kernel,
        out_shape=(
            jax.ShapeDtypeStruct((leaves * bands, BLOCK, BLOCK), jnp.float32),
            jax.ShapeDtypeStruct((leaves, BLOCK, BLOCK), jnp.float32),
        ),
        in_specs=[smem] * 4 + [vmem] * 4,
        out_specs=(anywhere, anywhere),
        scratch_shapes=[
            pltpu.VMEM((leaves, rows, BLOCK), jnp.float32),
            pltpu.SemaphoreType.DMA((leaves * bands,)),
            pltpu.SemaphoreType.DMA((leaves,)),
        ],
        name="schur_pieces",
    )(slot, live, piece, valid, cols, factor, inverse, blocks)


def place_kernel(slot_ref, base_ref, blocks_ref, out_ref):
    out_ref[...] = base_ref[...]

    def body(item, carry):
        slot = slot_ref[item]

        @pl.when(slot >= 0)
        def _():
            start = pl.multiple_of(slot * BLOCK, BLOCK)
            out_ref[pl.ds(start, BLOCK), :] += blocks_ref[item]

        return carry

    lax.fori_loop(0, blocks_ref.shape[0], body, 0)


def place_blocks(slots, base, blocks):
    vmem = pl.BlockSpec(memory_space=pltpu.VMEM)
    return pl.pallas_call(
        place_kernel,
        out_shape=jax.ShapeDtypeStruct(base.shape, jnp.float32),
        in_specs=[pl.BlockSpec(memory_space=pltpu.SMEM), vmem, vmem],
        out_specs=vmem,
        name="place_blocks",
    )(slots, base, blocks)


def locate(values, usable, count):
    hit = (values[..., None, :] == jnp.arange(count)[:, None]) & usable[..., None, :]
    index = jnp.sum(jnp.where(hit, jnp.arange(values.shape[-1]), 0), axis=-1)
    return index.astype(jnp.int32), jnp.any(hit, axis=-1)


def at(value, index, axis=0):
    return lax.dynamic_index_in_dim(value, index, axis, keepdims=False)


def swapped_core(along):
    other = lax.ppermute(along, "col_1", [(0, 1), (1, 0)])
    first = lax.axis_index("col_1") == 0
    both = jnp.stack([jnp.where(first, along, other), jnp.where(first, other, along)], axis=1)
    return both.reshape(-1, *along.shape[1:])


def from_first(value, axis, stride=None):
    index = lax.axis_index(axis)
    stride = stride or lax.axis_size(axis) // 2
    while stride:
        value = tree_round(value, axis, index, stride)
        stride //= 2
    return value


def tree_round(value, axis, index, stride):
    pairs = [(i, i + stride) for i in range(0, lax.axis_size(axis), 2 * stride)]
    other = lax.ppermute(value, axis, pairs)
    return jnp.where(index % (2 * stride) == stride, other, value)


def eliminate_and_assemble(child_front, parent_front, block_map):
    front = child_front[0]
    parent = parent_front[:, 0, 0, :]
    grid_rows = lax.axis_size("row")
    grid_cols = lax.axis_size(COL)
    leaves = lax.axis_size("leaf")
    row_id = lax.axis_index("row")
    col_id = lax.axis_index(COL)
    leaf_id = lax.axis_index("leaf")
    rows = front.shape[0]
    child_blocks = rows // BLOCK
    lead = PANEL // BLOCK

    padded = jnp.concatenate([jnp.full((leaves, lead), -1, jnp.int32), block_map], axis=1)
    maps = padded.reshape(leaves, grid_rows, child_blocks)
    usable = maps >= 0
    band = maps // grid_cols
    residue = maps % grid_cols
    lo_index, lo_valid = locate(residue, usable, grid_cols)
    hi_index, hi_valid = locate(band, usable, grid_rows)
    own_lo_index, own_lo_valid = at(lo_index, leaf_id), at(lo_valid, leaf_id)
    column_index = at(own_lo_index, col_id, 1)
    column_valid = at(own_lo_valid, col_id, 1)

    half = grid_rows // 2
    deal = exchange(front[:, :PANEL].reshape(grid_cols, -1, PANEL), COL)[0]
    parent_top = tree_round(parent[:PANEL], "row", row_id, half)
    send_index = at(own_lo_index, col_id)
    deal, send_index, parent_top = lax.optimization_barrier((deal, send_index, parent_top))
    picked = pick_columns(send_index, front)
    along = spread(deal, "col_0", lax.axis_size("col_0"))
    parent_top = tree_round(parent_top, "row", row_id, half // 2)
    along, parent_top = lax.optimization_barrier((along, parent_top))
    raw = swapped_core(along)
    parent_top = from_first(parent_top, "row", half // 4)
    picked, raw, parent_top = lax.optimization_barrier((picked, raw, parent_top))
    cols = exchange(picked, COL)
    raw = raw.reshape(rows, PANEL)
    mine = lax.dynamic_slice_in_dim(raw, at(column_index, row_id) * BLOCK, BLOCK, 0)
    blocks = lax.all_gather(mine, "row")
    inverse = lower_inverse(from_first(raw[:PANEL], "row"))
    factor = matmul_nt(raw, inverse)

    column_band = jnp.sum(
        jnp.where(jnp.arange(child_blocks) == column_index[:, None], at(band, leaf_id), 0), axis=-1
    )
    slot, slot_valid = locate(column_band, column_valid, leaves)
    pieces, tops = schur_pieces(
        slot,
        slot_valid.astype(jnp.int32),
        at(at(hi_index, leaf_id), row_id),
        at(at(hi_valid, leaf_id), row_id).astype(jnp.int32),
        cols,
        factor,
        inverse,
        blocks,
    )

    own_column = leaf_id * grid_cols + col_id
    present = jnp.any((maps == own_column) & usable, axis=(1, 2))
    row_slot = jnp.sum(
        jnp.where(jnp.arange(child_blocks) == hi_index[..., None], residue[:, :, None, :], 0),
        axis=-1,
    )
    row_slot = jnp.where(hi_valid & present[:, None, None], row_slot, -1).astype(jnp.int32)

    tops = exchange(tops.reshape(leaves * grid_rows, -1, BLOCK), LEAF_ROW)
    chosen = row_slot[:, :, 0].reshape(-1) == jnp.arange(lead)[:, None]
    top = jnp.sum(jnp.where(chosen[:, :, None, None], tops, 0.0), axis=1)
    top = spread(top, "row", grid_rows).transpose(1, 0, 2, 3).reshape(PANEL, BLOCK) + parent_top
    arrived = exchange(pieces, LEAF_ROW)

    every_leaf = lax.all_gather(top, "leaf")
    tops = lax.all_gather(at(every_leaf, row_id), COL)
    corner = from_first(every_leaf[0], "col_0")
    corner = lower_inverse(jnp.concatenate(list(swapped_core(corner[None])), axis=1))
    place = jnp.stack([row_id, own_column]).astype(jnp.int32)
    base = parent_base(place, corner, tops, top, parent)
    slots = jnp.where(own_column < lead, -1, at(row_slot, row_id, 2)).reshape(-1)
    result = place_blocks(slots, base, arrived)
    return (factor[None], result[:, None, None, :])


def solution(mesh):
    torus = Mesh(
        mesh.devices.reshape(mesh.shape["leaf"], mesh.shape["row"], 4, 2),
        ("leaf", "row", "col_0", "col_1"),
    )
    in_specs = (P("leaf", "row", COL), P("row", None, LEAF_COL, None), P())
    out_specs = (P("leaf", "row", None), P("row", None, LEAF_COL, None))
    return jax.shard_map(
        eliminate_and_assemble, mesh=torus, in_specs=in_specs, out_specs=out_specs, check_vma=False
    )
```

```python
import jax
import jax.numpy as jnp
from jax import lax
from jax.experimental import pallas as pl
from jax.experimental.pallas import tpu as pltpu
from jax.sharding import Mesh
from jax.sharding import PartitionSpec as P

PANEL = 256
BLOCK = 128
COL = ("col_0", "col_1")
LEAF_COL = ("leaf", "col_0", "col_1")
LEAF_ROW = ("leaf", "row")
HIGHEST = lax.Precision.HIGHEST
STEP = 64
GROUP = 8


def matmul(left, right):
    return jnp.dot(left, right, precision=HIGHEST, preferred_element_type=jnp.float32)


def matmul_nt(left, right):
    return lax.dot_general(
        left,
        right,
        (((1,), (1,)), ((), ())),
        precision=HIGHEST,
        preferred_element_type=jnp.float32,
    )


def matmul_tn(left, right):
    return lax.dot_general(
        left,
        right,
        (((0,), (0,)), ((), ())),
        precision=HIGHEST,
        preferred_element_type=jnp.float32,
    )


def exchange(value, axes):
    return lax.all_to_all(value, axes, split_axis=0, concat_axis=0, tiled=True)


def spread(value, axes, count):
    return exchange(jnp.broadcast_to(value[None], (count, *value.shape)), axes)


def eliminate(tile, eye, step):
    width = 2 * step
    row = lax.broadcasted_iota(jnp.int32, (step, width), 0)
    work = jnp.concatenate([tile, eye], axis=1)
    pivots = jnp.ones((step, width), jnp.float32)

    def tall(value):
        return jnp.concatenate([value] * (step // 8), axis=0)

    for first in range(0, step, GROUP):
        span = range(GROUP)
        cols = [
            jnp.broadcast_to(work[:, first + i : first + i + 1], (step, width)) for i in span
        ]
        rows = [jnp.broadcast_to(work[first + i : first + i + 1, :], (8, width)) for i in span]
        small = {}
        for i in span:
            for j in range(i, GROUP):
                small[i, j] = jnp.broadcast_to(cols[i][first + j : first + j + 1, :], (8, width))
        ratio = {}
        recip = []
        for i in span:
            recip.append(1.0 / small[i, i])
            for j in range(i + 1, GROUP):
                ratio[i, j] = small[i, j] * recip[i]
            for j in range(i + 1, GROUP):
                for k in range(j, GROUP):
                    small[j, k] = small[j, k] - ratio[i, j] * small[i, k]
        update = None
        for i in span:
            scaled = jnp.where(row > first + i, cols[i] * tall(recip[i]), 0.0)
            pivots = jnp.where(row == first + i, tall(small[i, i]), pivots)
            for j in range(i + 1, GROUP):
                cols[j] = cols[j] - cols[i] * tall(ratio[i, j])
                rows[j] = rows[j] - ratio[i, j] * rows[i]
            term = scaled * tall(rows[i])
            update = term if update is None else update + term
        work = work - update
    return work[:, step:width] * lax.rsqrt(pivots)[:, :step]


def invert(corner, out_ref, work_ref):
    size = corner.shape[0]
    step = STEP
    row = lax.broadcasted_iota(jnp.int32, (size, size), 0)
    col = lax.broadcasted_iota(jnp.int32, (size, size), 1)
    work_ref[:, :size] = corner
    work_ref[:, size:] = (row == col).astype(jnp.float32)
    small_row = lax.broadcasted_iota(jnp.int32, (step, step), 0)
    small_col = lax.broadcasted_iota(jnp.int32, (step, step), 1)
    eye = (small_row == small_col).astype(jnp.float32)
    for start in range(0, size, step):
        stop = start + step
        lead = eliminate(work_ref[start:stop, start:stop], eye, step)
        upper = matmul(lead, work_ref[start:stop, :])
        out_ref[start:stop, :] = upper[:, size:]
        if stop < size:
            work_ref[stop:, :] = work_ref[stop:, :] - matmul_tn(upper[:, stop:size], upper)


def inverse_kernel(lower_ref, out_ref, work_ref):
    side = lower_ref.shape[1]
    below = lower_ref[side : 2 * side, :]
    top = jnp.concatenate([lower_ref[:side, :], below.T], axis=1)
    bottom = jnp.concatenate([below, lower_ref[2 * side :, :]], axis=1)
    invert(jnp.concatenate([top, bottom], axis=0), out_ref, work_ref)


def lower_inverse(lower):
    size = 2 * lower.shape[1]
    return pl.pallas_call(
        inverse_kernel,
        out_shape=jax.ShapeDtypeStruct((size, size), jnp.float32),
        scratch_shapes=[pltpu.VMEM((size, 2 * size), jnp.float32)],
        name="lower_inverse",
    )(lower)


def parent_kernel(where_ref, inverse_ref, tops_ref, top_ref, parent_ref, out_ref):
    row_id, own_column = where_ref[0], where_ref[1]
    lead = PANEL // BLOCK
    blocks = tops_ref.shape[0]

    @pl.when(own_column >= lead)
    def _():
        upper = matmul(inverse_ref[...], top_ref[...])

        def body(block, carry):
            part = pl.ds(pl.multiple_of(block * BLOCK, BLOCK), BLOCK)
            change = matmul_tn(matmul(inverse_ref[...], tops_ref[block]), upper)
            first = (row_id == 0) & (block < lead)
            out_ref[part, :] = parent_ref[part, :] - jnp.where(first, 0.0, change)
            return carry

        lax.fori_loop(0, blocks, body, 0)

    @pl.when(own_column < lead)
    def _():
        start = pl.multiple_of(jnp.minimum(own_column, lead - 1) * BLOCK, BLOCK)
        rows = inverse_ref[pl.ds(start, BLOCK), :]

        def body(block, carry):
            part = pl.ds(pl.multiple_of(block * BLOCK, BLOCK), BLOCK)
            out_ref[part, :] = matmul(rows, tops_ref[block]).T
            return carry

        lax.fori_loop(0, blocks, body, 0)


def parent_base(where, inverse, tops, top, parent):
    vmem = pl.BlockSpec(memory_space=pltpu.VMEM)
    return pl.pallas_call(
        parent_kernel,
        out_shape=jax.ShapeDtypeStruct(parent.shape, jnp.float32),
        in_specs=[pl.BlockSpec(memory_space=pltpu.SMEM), vmem, vmem, vmem, vmem],
        out_specs=vmem,
        name="parent_base",
    )(where, inverse, tops, top, parent)


def pick_kernel(index_ref, front_ref, out_ref):
    out_ref[0] = front_ref[...]


def pick_columns(index, front):
    rows = front.shape[0]
    count = index.shape[0]
    return pl.pallas_call(
        pick_kernel,
        out_shape=jax.ShapeDtypeStruct((count, rows, BLOCK), jnp.float32),
        grid_spec=pltpu.PrefetchScalarGridSpec(
            num_scalar_prefetch=1,
            grid=(count,),
            in_specs=[pl.BlockSpec((rows, BLOCK), lambda i, index: (0, index[i]))],
            out_specs=pl.BlockSpec((1, rows, BLOCK), lambda i, index: (i, 0, 0)),
        ),
        name="pick_columns",
    )(index, front)


def schur_kernel(
    slot_ref, live_ref, piece_ref, valid_ref, cols_ref, factor_ref, inverse_ref, block_ref,
    out_ref, tmp_ref, sems,
):
    leaves = live_ref.shape[0]
    bands = valid_ref.shape[0]

    def copy(leaf, dest):
        start = pl.multiple_of(piece_ref[dest] * BLOCK, BLOCK)
        piece = tmp_ref.at[leaf, pl.ds(start, BLOCK), :]
        item = leaf * bands + dest
        return pltpu.make_async_copy(piece, out_ref.at[item], sems.at[item])

    def each(leaf, act):
        for dest in range(bands):

            @pl.when(valid_ref[dest] > 0)
            def _(dest=dest):
                act(copy(leaf, dest))

    def start(leaf, carry):
        @pl.when(live_ref[leaf] > 0)
        def _():
            slot = slot_ref[leaf]
            block = matmul_nt(block_ref[slot], inverse_ref[...])
            tmp_ref[leaf] = cols_ref[slot] - matmul_nt(factor_ref[...], block)
            each(leaf, lambda copy: copy.start())

        return carry

    def finish(leaf, carry):
        @pl.when(live_ref[leaf] > 0)
        def _():
            each(leaf, lambda copy: copy.wait())

        return carry

    lax.fori_loop(0, leaves, start, 0)
    lax.fori_loop(0, leaves, finish, 0)


def schur_pieces(slot, live, piece, valid, cols, factor, inverse, blocks):
    leaves = slot.shape[0]
    bands = piece.shape[0]
    rows = factor.shape[0]
    smem = pl.BlockSpec(memory_space=pltpu.SMEM)
    vmem = pl.BlockSpec(memory_space=pltpu.VMEM)
    anywhere = pl.BlockSpec(memory_space=pl.ANY)
    return pl.pallas_call(
        schur_kernel,
        out_shape=jax.ShapeDtypeStruct((leaves * bands, BLOCK, BLOCK), jnp.float32),
        in_specs=[smem] * 4 + [vmem] * 4,
        out_specs=anywhere,
        scratch_shapes=[
            pltpu.VMEM((leaves, rows, BLOCK), jnp.float32),
            pltpu.SemaphoreType.DMA((leaves * bands,)),
        ],
        name="schur_pieces",
    )(slot, live, piece, valid, cols, factor, inverse, blocks)


def top_kernel(slot_ref, live_ref, row_ref, cols_ref, raw_ref, inverse_ref, block_ref, out_ref):
    @pl.when(row_ref[1] > 0)
    def _():
        part = pl.ds(pl.multiple_of(row_ref[0] * BLOCK, BLOCK), BLOCK)
        factor = matmul_nt(raw_ref[part, :], inverse_ref[...])

        def body(leaf, carry):
            @pl.when(live_ref[leaf] > 0)
            def _():
                slot = slot_ref[leaf]
                block = matmul_nt(block_ref[slot], inverse_ref[...])
                out_ref[leaf] = cols_ref[slot, part, :] - matmul_nt(factor, block)

            return carry

        lax.fori_loop(0, live_ref.shape[0], body, 0)


def top_pieces(slot, live, row, cols, raw, inverse, blocks):
    smem = pl.BlockSpec(memory_space=pltpu.SMEM)
    vmem = pl.BlockSpec(memory_space=pltpu.VMEM)
    return pl.pallas_call(
        top_kernel,
        out_shape=jax.ShapeDtypeStruct((slot.shape[0], BLOCK, BLOCK), jnp.float32),
        in_specs=[smem] * 3 + [vmem] * 4,
        out_specs=vmem,
        name="top_pieces",
    )(slot, live, row, cols, raw, inverse, blocks)


def place_kernel(slot_ref, base_ref, blocks_ref, out_ref):
    out_ref[...] = base_ref[...]

    def body(item, carry):
        slot = slot_ref[item]

        @pl.when(slot >= 0)
        def _():
            start = pl.multiple_of(slot * BLOCK, BLOCK)
            out_ref[pl.ds(start, BLOCK), :] += blocks_ref[item]

        return carry

    lax.fori_loop(0, blocks_ref.shape[0], body, 0)


def place_blocks(slots, base, blocks):
    vmem = pl.BlockSpec(memory_space=pltpu.VMEM)
    return pl.pallas_call(
        place_kernel,
        out_shape=jax.ShapeDtypeStruct(base.shape, jnp.float32),
        in_specs=[pl.BlockSpec(memory_space=pltpu.SMEM), vmem, vmem],
        out_specs=vmem,
        name="place_blocks",
    )(slots, base, blocks)


def locate(values, usable, count):
    hit = (values[..., None, :] == jnp.arange(count)[:, None]) & usable[..., None, :]
    index = jnp.sum(jnp.where(hit, jnp.arange(values.shape[-1]), 0), axis=-1)
    return index.astype(jnp.int32), jnp.any(hit, axis=-1)


def at(value, index, axis=0):
    return lax.dynamic_index_in_dim(value, index, axis, keepdims=False)


def swapped_core(along):
    other = lax.ppermute(along, "col_1", [(0, 1), (1, 0)])
    first = lax.axis_index("col_1") == 0
    both = jnp.stack([jnp.where(first, along, other), jnp.where(first, other, along)], axis=1)
    return both.reshape(-1, *along.shape[1:])


def from_first(value, axis, stride=None):
    index = lax.axis_index(axis)
    stride = stride or lax.axis_size(axis) // 2
    while stride:
        value = tree_round(value, axis, index, stride)
        stride //= 2
    return value


def tree_round(value, axis, index, stride):
    pairs = [(i, i + stride) for i in range(0, lax.axis_size(axis), 2 * stride)]
    other = lax.ppermute(value, axis, pairs)
    return jnp.where(index % (2 * stride) == stride, other, value)


def eliminate_and_assemble(child_front, parent_front, block_map):
    front = child_front[0]
    parent = parent_front[:, 0, 0, :]
    grid_rows = lax.axis_size("row")
    grid_cols = lax.axis_size(COL)
    leaves = lax.axis_size("leaf")
    row_id = lax.axis_index("row")
    col_id = lax.axis_index(COL)
    leaf_id = lax.axis_index("leaf")
    rows = front.shape[0]
    child_blocks = rows // BLOCK
    lead = PANEL // BLOCK

    padded = jnp.concatenate([jnp.full((leaves, lead), -1, jnp.int32), block_map], axis=1)
    maps = padded.reshape(leaves, grid_rows, child_blocks)
    usable = maps >= 0
    band = maps // grid_cols
    residue = maps % grid_cols
    lo_index, lo_valid = locate(residue, usable, grid_cols)
    hi_index, hi_valid = locate(band, usable, grid_rows)
    own_lo_index, own_lo_valid = at(lo_index, leaf_id), at(lo_valid, leaf_id)
    column_index = at(own_lo_index, col_id, 1)
    column_valid = at(own_lo_valid, col_id, 1)

    half = grid_rows // 2
    deal = exchange(front[:, :PANEL].reshape(grid_cols, -1, PANEL), COL)[0]
    parent_top = tree_round(parent[:PANEL], "row", row_id, half)
    send_index = at(own_lo_index, col_id)
    deal, send_index, parent_top = lax.optimization_barrier((deal, send_index, parent_top))
    picked = pick_columns(send_index, front)
    along = spread(deal, "col_0", lax.axis_size("col_0"))
    parent_top = tree_round(parent_top, "row", row_id, half // 2)
    along, parent_top = lax.optimization_barrier((along, parent_top))
    raw = swapped_core(along)
    parent_top = from_first(parent_top, "row", half // 4)
    picked, raw, parent_top = lax.optimization_barrier((picked, raw, parent_top))
    cols = exchange(picked, COL)
    raw = raw.reshape(rows, PANEL)
    mine = lax.dynamic_slice_in_dim(raw, at(column_index, row_id) * BLOCK, BLOCK, 0)
    blocks = lax.all_gather(mine, "row")
    corner = jnp.concatenate([raw[:PANEL, :BLOCK], raw[BLOCK:PANEL, BLOCK:]])
    inverse = lower_inverse(from_first(corner, "row"))
    column_band = jnp.sum(
        jnp.where(jnp.arange(child_blocks) == column_index[:, None], at(band, leaf_id), 0), axis=-1
    )
    slot, slot_valid = locate(column_band, column_valid, leaves)
    live = slot_valid.astype(jnp.int32)
    piece = at(at(hi_index, leaf_id), row_id)
    valid = at(at(hi_valid, leaf_id), row_id)
    first = jnp.sum(
        jnp.where(jnp.arange(child_blocks) == piece[0], at(at(residue, leaf_id), row_id), 0)
    )
    row = jnp.stack([piece[0], (valid[0] & (first < lead)).astype(jnp.int32)])
    tops = top_pieces(slot, live, row, cols, raw, inverse, blocks)
    factor = matmul_nt(raw, inverse)
    pieces = schur_pieces(slot, live, piece, valid.astype(jnp.int32), cols, factor, inverse, blocks)

    own_column = leaf_id * grid_cols + col_id
    present = jnp.any((maps == own_column) & usable, axis=(1, 2))
    row_slot = jnp.sum(
        jnp.where(jnp.arange(child_blocks) == hi_index[..., None], residue[:, :, None, :], 0),
        axis=-1,
    )
    row_slot = jnp.where(hi_valid & present[:, None, None], row_slot, -1).astype(jnp.int32)

    tops = exchange(tops.reshape(leaves * grid_rows, -1, BLOCK), LEAF_ROW)
    chosen = row_slot[:, :, 0].reshape(-1) == jnp.arange(lead)[:, None]
    top = jnp.sum(jnp.where(chosen[:, :, None, None], tops, 0.0), axis=1)
    top = spread(top, "row", grid_rows).transpose(1, 0, 2, 3).reshape(PANEL, BLOCK) + parent_top
    arrived = exchange(pieces, LEAF_ROW)

    every_leaf = lax.all_gather(top, "leaf")
    tops = lax.all_gather(at(every_leaf, row_id), COL)
    corner = from_first(every_leaf[0], "col_0")
    corner = swapped_core(corner[None])
    corner = lower_inverse(jnp.concatenate([corner[0], corner[1, BLOCK:]]))
    place = jnp.stack([row_id, own_column]).astype(jnp.int32)
    base = parent_base(place, corner, tops, top, parent)
    slots = jnp.where(own_column < lead, -1, at(row_slot, row_id, 2)).reshape(-1)
    result = place_blocks(slots, base, arrived)
    return (factor[None], result[:, None, None, :])


def solution(mesh):
    torus = Mesh(
        mesh.devices.reshape(mesh.shape["leaf"], mesh.shape["row"], 4, 2),
        ("leaf", "row", "col_0", "col_1"),
    )
    in_specs = (P("leaf", "row", COL), P("row", None, LEAF_COL, None), P())
    out_specs = (P("leaf", "row", None), P("row", None, LEAF_COL, None))
    return jax.shard_map(
        eliminate_and_assemble, mesh=torus, in_specs=in_specs, out_specs=out_specs, check_vma=False
    )
```

```python
import jax
import jax.numpy as jnp
from jax import lax
from jax.experimental import pallas as pl
from jax.experimental.pallas import tpu as pltpu
from jax.sharding import Mesh
from jax.sharding import PartitionSpec as P

PANEL = 256
BLOCK = 128
COL = ("col_0", "col_1")
LEAF_COL = ("leaf", "col_0", "col_1")
LEAF_ROW = ("leaf", "row")
HIGHEST = lax.Precision.HIGHEST
STEP = 64
GROUP = 8


def matmul(left, right):
    return jnp.dot(left, right, precision=HIGHEST, preferred_element_type=jnp.float32)


def matmul_nt(left, right):
    return lax.dot_general(
        left,
        right,
        (((1,), (1,)), ((), ())),
        precision=HIGHEST,
        preferred_element_type=jnp.float32,
    )


def matmul_tn(left, right):
    return lax.dot_general(
        left,
        right,
        (((0,), (0,)), ((), ())),
        precision=HIGHEST,
        preferred_element_type=jnp.float32,
    )


def exchange(value, axes):
    return lax.all_to_all(value, axes, split_axis=0, concat_axis=0, tiled=True)


def spread(value, axes, count):
    return exchange(jnp.broadcast_to(value[None], (count, *value.shape)), axes)


def eliminate(tile, eye, step):
    width = 2 * step
    row = lax.broadcasted_iota(jnp.int32, (step, width), 0)
    work = jnp.concatenate([tile, eye], axis=1)
    pivots = jnp.ones((step, width), jnp.float32)

    def tall(value):
        return jnp.concatenate([value] * (step // 8), axis=0)

    for first in range(0, step, GROUP):
        span = range(GROUP)
        cols = [
            jnp.broadcast_to(work[:, first + i : first + i + 1], (step, width)) for i in span
        ]
        rows = [jnp.broadcast_to(work[first + i : first + i + 1, :], (8, width)) for i in span]
        small = {}
        for i in span:
            for j in range(i, GROUP):
                small[i, j] = jnp.broadcast_to(cols[i][first + j : first + j + 1, :], (8, width))
        ratio = {}
        recip = []
        for i in span:
            recip.append(1.0 / small[i, i])
            for j in range(i + 1, GROUP):
                ratio[i, j] = small[i, j] * recip[i]
            for j in range(i + 1, GROUP):
                for k in range(j, GROUP):
                    small[j, k] = small[j, k] - ratio[i, j] * small[i, k]
        update = None
        for i in span:
            scaled = jnp.where(row > first + i, cols[i] * tall(recip[i]), 0.0)
            pivots = jnp.where(row == first + i, tall(small[i, i]), pivots)
            for j in range(i + 1, GROUP):
                cols[j] = cols[j] - cols[i] * tall(ratio[i, j])
                rows[j] = rows[j] - ratio[i, j] * rows[i]
            term = scaled * tall(rows[i])
            update = term if update is None else update + term
        work = work - update
    return work[:, step:width] * lax.rsqrt(pivots)[:, :step]


def invert(corner, out_ref, work_ref):
    size = corner.shape[0]
    step = STEP
    row = lax.broadcasted_iota(jnp.int32, (size, size), 0)
    col = lax.broadcasted_iota(jnp.int32, (size, size), 1)
    work_ref[:, :size] = corner
    work_ref[:, size:] = (row == col).astype(jnp.float32)
    small_row = lax.broadcasted_iota(jnp.int32, (step, step), 0)
    small_col = lax.broadcasted_iota(jnp.int32, (step, step), 1)
    eye = (small_row == small_col).astype(jnp.float32)
    for start in range(0, size, step):
        stop = start + step
        lead = eliminate(work_ref[start:stop, start:stop], eye, step)
        upper = matmul(lead, work_ref[start:stop, :])
        out_ref[start:stop, :] = upper[:, size:]
        if stop < size:
            work_ref[stop:, :] = work_ref[stop:, :] - matmul_tn(upper[:, stop:size], upper)


def inverse_kernel(lower_ref, out_ref, work_ref):
    side = lower_ref.shape[1]
    below = lower_ref[side : 2 * side, :]
    top = jnp.concatenate([lower_ref[:side, :], below.T], axis=1)
    bottom = jnp.concatenate([below, lower_ref[2 * side :, :]], axis=1)
    invert(jnp.concatenate([top, bottom], axis=0), out_ref, work_ref)


def lower_inverse(lower):
    size = 2 * lower.shape[1]
    return pl.pallas_call(
        inverse_kernel,
        out_shape=jax.ShapeDtypeStruct((size, size), jnp.float32),
        scratch_shapes=[pltpu.VMEM((size, 2 * size), jnp.float32)],
        name="lower_inverse",
    )(lower)


def parent_kernel(where_ref, inverse_ref, tops_ref, top_ref, parent_ref, out_ref):
    row_id, own_column = where_ref[0], where_ref[1]
    lead = PANEL // BLOCK
    blocks = tops_ref.shape[0]

    @pl.when(own_column >= lead)
    def _():
        upper = matmul(inverse_ref[...], top_ref[...])

        def body(block, carry):
            part = pl.ds(pl.multiple_of(block * BLOCK, BLOCK), BLOCK)
            change = matmul_tn(matmul(inverse_ref[...], tops_ref[block]), upper)
            first = (row_id == 0) & (block < lead)
            out_ref[part, :] = parent_ref[part, :] - jnp.where(first, 0.0, change)
            return carry

        lax.fori_loop(0, blocks, body, 0)

    @pl.when(own_column < lead)
    def _():
        start = pl.multiple_of(jnp.minimum(own_column, lead - 1) * BLOCK, BLOCK)
        rows = inverse_ref[pl.ds(start, BLOCK), :]

        def body(block, carry):
            part = pl.ds(pl.multiple_of(block * BLOCK, BLOCK), BLOCK)
            out_ref[part, :] = matmul(rows, tops_ref[block]).T
            return carry

        lax.fori_loop(0, blocks, body, 0)


def parent_base(where, inverse, tops, top, parent):
    vmem = pl.BlockSpec(memory_space=pltpu.VMEM)
    return pl.pallas_call(
        parent_kernel,
        out_shape=jax.ShapeDtypeStruct(parent.shape, jnp.float32),
        in_specs=[pl.BlockSpec(memory_space=pltpu.SMEM), vmem, vmem, vmem, vmem],
        out_specs=vmem,
        name="parent_base",
    )(where, inverse, tops, top, parent)


def pick_kernel(index_ref, front_ref, out_ref):
    out_ref[0] = front_ref[...]


def pick_columns(index, front):
    rows = front.shape[0]
    count = index.shape[0]
    return pl.pallas_call(
        pick_kernel,
        out_shape=jax.ShapeDtypeStruct((count, rows, BLOCK), jnp.float32),
        grid_spec=pltpu.PrefetchScalarGridSpec(
            num_scalar_prefetch=1,
            grid=(count,),
            in_specs=[pl.BlockSpec((rows, BLOCK), lambda i, index: (0, index[i]))],
            out_specs=pl.BlockSpec((1, rows, BLOCK), lambda i, index: (i, 0, 0)),
        ),
        name="pick_columns",
    )(index, front)


def schur_kernel(
    slot_ref, live_ref, piece_ref, valid_ref, cols_ref, factor_ref, inverse_ref, block_ref,
    out_ref, tmp_ref, sems,
):
    leaves = live_ref.shape[0]
    bands = valid_ref.shape[0]

    def copy(leaf, dest):
        start = pl.multiple_of(piece_ref[dest] * BLOCK, BLOCK)
        piece = tmp_ref.at[leaf, pl.ds(start, BLOCK), :]
        item = leaf * bands + dest
        return pltpu.make_async_copy(piece, out_ref.at[item], sems.at[item])

    def each(leaf, act):
        for dest in range(bands):

            @pl.when(valid_ref[dest] > 0)
            def _(dest=dest):
                act(copy(leaf, dest))

    def start(leaf, carry):
        @pl.when(live_ref[leaf] > 0)
        def _():
            slot = slot_ref[leaf]
            block = matmul_nt(block_ref[slot], inverse_ref[...])
            tmp_ref[leaf] = cols_ref[slot] - matmul_nt(factor_ref[...], block)
            each(leaf, lambda copy: copy.start())

        return carry

    def finish(leaf, carry):
        @pl.when(live_ref[leaf] > 0)
        def _():
            each(leaf, lambda copy: copy.wait())

        return carry

    lax.fori_loop(0, leaves, start, 0)
    lax.fori_loop(0, leaves, finish, 0)


def schur_pieces(slot, live, piece, valid, cols, factor, inverse, blocks):
    leaves = slot.shape[0]
    bands = piece.shape[0]
    rows = factor.shape[0]
    smem = pl.BlockSpec(memory_space=pltpu.SMEM)
    vmem = pl.BlockSpec(memory_space=pltpu.VMEM)
    anywhere = pl.BlockSpec(memory_space=pl.ANY)
    return pl.pallas_call(
        schur_kernel,
        out_shape=jax.ShapeDtypeStruct((leaves * bands, BLOCK, BLOCK), jnp.float32),
        in_specs=[smem] * 4 + [vmem] * 4,
        out_specs=anywhere,
        scratch_shapes=[
            pltpu.VMEM((leaves, rows, BLOCK), jnp.float32),
            pltpu.SemaphoreType.DMA((leaves * bands,)),
        ],
        name="schur_pieces",
    )(slot, live, piece, valid, cols, factor, inverse, blocks)


def top_kernel(slot_ref, live_ref, row_ref, cols_ref, raw_ref, inverse_ref, block_ref, out_ref):
    @pl.when(row_ref[1] > 0)
    def _():
        part = pl.ds(pl.multiple_of(row_ref[0] * BLOCK, BLOCK), BLOCK)
        factor = matmul_nt(raw_ref[part, :], inverse_ref[...])

        def body(leaf, carry):
            @pl.when(live_ref[leaf] > 0)
            def _():
                slot = slot_ref[leaf]
                block = matmul_nt(block_ref[slot], inverse_ref[...])
                out_ref[leaf] = cols_ref[slot, part, :] - matmul_nt(factor, block)

            return carry

        lax.fori_loop(0, live_ref.shape[0], body, 0)


def top_pieces(slot, live, row, cols, raw, inverse, blocks):
    smem = pl.BlockSpec(memory_space=pltpu.SMEM)
    vmem = pl.BlockSpec(memory_space=pltpu.VMEM)
    return pl.pallas_call(
        top_kernel,
        out_shape=jax.ShapeDtypeStruct((slot.shape[0], BLOCK, BLOCK), jnp.float32),
        in_specs=[smem] * 3 + [vmem] * 4,
        out_specs=vmem,
        name="top_pieces",
    )(slot, live, row, cols, raw, inverse, blocks)


def place_kernel(slot_ref, base_ref, blocks_ref, out_ref, tmp_ref, sems):
    def copy(item):
        return pltpu.make_async_copy(blocks_ref.at[item], tmp_ref.at[item], sems.at[item])

    def start(item, carry):
        @pl.when(slot_ref[item] >= 0)
        def _():
            copy(item).start()

        return carry

    def finish(item, carry):
        slot = slot_ref[item]

        @pl.when(slot >= 0)
        def _():
            copy(item).wait()
            first = pl.multiple_of(slot * BLOCK, BLOCK)
            out_ref[pl.ds(first, BLOCK), :] += tmp_ref[item]

        return carry

    count = blocks_ref.shape[0]
    lax.fori_loop(0, count, start, 0)
    out_ref[...] = base_ref[...]
    lax.fori_loop(0, count, finish, 0)


def place_blocks(slots, base, blocks):
    vmem = pl.BlockSpec(memory_space=pltpu.VMEM)
    return pl.pallas_call(
        place_kernel,
        out_shape=jax.ShapeDtypeStruct(base.shape, jnp.float32),
        in_specs=[
            pl.BlockSpec(memory_space=pltpu.SMEM),
            vmem,
            pl.BlockSpec(memory_space=pl.ANY),
        ],
        out_specs=vmem,
        scratch_shapes=[
            pltpu.VMEM(blocks.shape, jnp.float32),
            pltpu.SemaphoreType.DMA((blocks.shape[0],)),
        ],
        name="place_blocks",
    )(slots, base, blocks)


def locate(values, usable, count):
    hit = (values[..., None, :] == jnp.arange(count)[:, None]) & usable[..., None, :]
    index = jnp.sum(jnp.where(hit, jnp.arange(values.shape[-1]), 0), axis=-1)
    return index.astype(jnp.int32), jnp.any(hit, axis=-1)


def at(value, index, axis=0):
    return lax.dynamic_index_in_dim(value, index, axis, keepdims=False)


def swapped_core(along):
    other = lax.ppermute(along, "col_1", [(0, 1), (1, 0)])
    first = lax.axis_index("col_1") == 0
    both = jnp.stack([jnp.where(first, along, other), jnp.where(first, other, along)], axis=1)
    return both.reshape(-1, *along.shape[1:])


def from_first(value, axis, stride=None):
    index = lax.axis_index(axis)
    stride = stride or lax.axis_size(axis) // 2
    while stride:
        value = tree_round(value, axis, index, stride)
        stride //= 2
    return value


def tree_round(value, axis, index, stride):
    pairs = [(i, i + stride) for i in range(0, lax.axis_size(axis), 2 * stride)]
    other = lax.ppermute(value, axis, pairs)
    return jnp.where(index % (2 * stride) == stride, other, value)


def eliminate_and_assemble(child_front, parent_front, block_map):
    front = child_front[0]
    parent = parent_front[:, 0, 0, :]
    grid_rows = lax.axis_size("row")
    grid_cols = lax.axis_size(COL)
    leaves = lax.axis_size("leaf")
    row_id = lax.axis_index("row")
    col_id = lax.axis_index(COL)
    leaf_id = lax.axis_index("leaf")
    rows = front.shape[0]
    child_blocks = rows // BLOCK
    lead = PANEL // BLOCK

    padded = jnp.concatenate([jnp.full((leaves, lead), -1, jnp.int32), block_map], axis=1)
    maps = padded.reshape(leaves, grid_rows, child_blocks)
    usable = maps >= 0
    band = maps // grid_cols
    residue = maps % grid_cols
    lo_index, lo_valid = locate(residue, usable, grid_cols)
    hi_index, hi_valid = locate(band, usable, grid_rows)
    own_lo_index, own_lo_valid = at(lo_index, leaf_id), at(lo_valid, leaf_id)
    column_index = at(own_lo_index, col_id, 1)
    column_valid = at(own_lo_valid, col_id, 1)

    half = grid_rows // 2
    deal = exchange(front[:, :PANEL].reshape(grid_cols, -1, PANEL), COL)[0]
    parent_top = tree_round(parent[:PANEL], "row", row_id, half)
    send_index = at(own_lo_index, col_id)
    deal, send_index, parent_top = lax.optimization_barrier((deal, send_index, parent_top))
    picked = pick_columns(send_index, front)
    along = spread(deal, "col_0", lax.axis_size("col_0"))
    parent_top = tree_round(parent_top, "row", row_id, half // 2)
    along, parent_top = lax.optimization_barrier((along, parent_top))
    raw = swapped_core(along)
    parent_top = from_first(parent_top, "row", half // 4)
    picked, raw, parent_top = lax.optimization_barrier((picked, raw, parent_top))
    cols = exchange(picked, COL)
    raw = raw.reshape(rows, PANEL)
    mine = lax.dynamic_slice_in_dim(raw, at(column_index, row_id) * BLOCK, BLOCK, 0)
    blocks = lax.all_gather(mine, "row")
    corner = jnp.concatenate([raw[:PANEL, :BLOCK], raw[BLOCK:PANEL, BLOCK:]])
    inverse = lower_inverse(from_first(corner, "row"))
    column_band = jnp.sum(
        jnp.where(jnp.arange(child_blocks) == column_index[:, None], at(band, leaf_id), 0), axis=-1
    )
    slot, slot_valid = locate(column_band, column_valid, leaves)
    live = slot_valid.astype(jnp.int32)
    piece = at(at(hi_index, leaf_id), row_id)
    valid = at(at(hi_valid, leaf_id), row_id)
    first = jnp.sum(
        jnp.where(jnp.arange(child_blocks) == piece[0], at(at(residue, leaf_id), row_id), 0)
    )
    row = jnp.stack([piece[0], (valid[0] & (first < lead)).astype(jnp.int32)])
    tops = top_pieces(slot, live, row, cols, raw, inverse, blocks)
    factor = matmul_nt(raw, inverse)
    pieces = schur_pieces(slot, live, piece, valid.astype(jnp.int32), cols, factor, inverse, blocks)

    own_column = leaf_id * grid_cols + col_id
    present = jnp.any((maps == own_column) & usable, axis=(1, 2))
    row_slot = jnp.sum(
        jnp.where(jnp.arange(child_blocks) == hi_index[..., None], residue[:, :, None, :], 0),
        axis=-1,
    )
    row_slot = jnp.where(hi_valid & present[:, None, None], row_slot, -1).astype(jnp.int32)

    tops = exchange(tops.reshape(leaves * grid_rows, -1, BLOCK), LEAF_ROW)
    chosen = row_slot[:, :, 0].reshape(-1) == jnp.arange(lead)[:, None]
    top = jnp.sum(jnp.where(chosen[:, :, None, None], tops, 0.0), axis=1)
    top = spread(top, "row", grid_rows).transpose(1, 0, 2, 3).reshape(PANEL, BLOCK) + parent_top
    arrived = exchange(pieces, LEAF_ROW)

    every_leaf = lax.all_gather(top, "leaf")
    tops = lax.all_gather(at(every_leaf, row_id), COL)
    corner = from_first(every_leaf[0], "col_0")
    corner = swapped_core(corner[None])
    corner = lower_inverse(jnp.concatenate([corner[0], corner[1, BLOCK:]]))
    place = jnp.stack([row_id, own_column]).astype(jnp.int32)
    base = parent_base(place, corner, tops, top, parent)
    slots = jnp.where(own_column < lead, -1, at(row_slot, row_id, 2)).reshape(-1)
    result = place_blocks(slots, base, arrived)
    return (factor[None], result[:, None, None, :])


def solution(mesh):
    torus = Mesh(
        mesh.devices.reshape(mesh.shape["leaf"], mesh.shape["row"], 4, 2),
        ("leaf", "row", "col_0", "col_1"),
    )
    in_specs = (P("leaf", "row", COL), P("row", None, LEAF_COL, None), P())
    out_specs = (P("leaf", "row", None), P("row", None, LEAF_COL, None))
    return jax.shard_map(
        eliminate_and_assemble, mesh=torus, in_specs=in_specs, out_specs=out_specs, check_vma=False
    )
```

```python
import jax
import jax.numpy as jnp
from jax import lax
from jax.experimental import pallas as pl
from jax.experimental.pallas import tpu as pltpu
from jax.sharding import Mesh
from jax.sharding import PartitionSpec as P

PANEL = 256
BLOCK = 128
COL = ("col_0", "col_1")
LEAF_COL = ("leaf", "col_0", "col_1")
LEAF_ROW = ("leaf", "row")
HIGHEST = lax.Precision.HIGHEST
HIGH = lax.Precision.HIGH
STEP = 64
GROUP = 8


def matmul(left, right, precision=HIGHEST):
    return jnp.dot(left, right, precision=precision, preferred_element_type=jnp.float32)


def matmul_nt(left, right):
    return lax.dot_general(
        left,
        right,
        (((1,), (1,)), ((), ())),
        precision=HIGHEST,
        preferred_element_type=jnp.float32,
    )


def matmul_tn(left, right, precision=HIGHEST):
    return lax.dot_general(
        left,
        right,
        (((0,), (0,)), ((), ())),
        precision=precision,
        preferred_element_type=jnp.float32,
    )


def exchange(value, axes):
    return lax.all_to_all(value, axes, split_axis=0, concat_axis=0, tiled=True)


def spread(value, axes, count):
    return exchange(jnp.broadcast_to(value[None], (count, *value.shape)), axes)


def eliminate(tile, eye, step):
    width = 2 * step
    row = lax.broadcasted_iota(jnp.int32, (step, width), 0)
    work = jnp.concatenate([tile, eye], axis=1)
    pivots = jnp.ones((step, width), jnp.float32)

    def tall(value):
        return jnp.concatenate([value] * (step // 8), axis=0)

    for first in range(0, step, GROUP):
        span = range(GROUP)
        cols = [
            jnp.broadcast_to(work[:, first + i : first + i + 1], (step, width)) for i in span
        ]
        rows = [jnp.broadcast_to(work[first + i : first + i + 1, :], (8, width)) for i in span]
        small = {}
        for i in span:
            for j in range(i, GROUP):
                small[i, j] = jnp.broadcast_to(cols[i][first + j : first + j + 1, :], (8, width))
        ratio = {}
        recip = []
        for i in span:
            recip.append(1.0 / small[i, i])
            for j in range(i + 1, GROUP):
                ratio[i, j] = small[i, j] * recip[i]
            for j in range(i + 1, GROUP):
                for k in range(j, GROUP):
                    small[j, k] = small[j, k] - ratio[i, j] * small[i, k]
        update = None
        for i in span:
            scaled = jnp.where(row > first + i, cols[i] * tall(recip[i]), 0.0)
            pivots = jnp.where(row == first + i, tall(small[i, i]), pivots)
            for j in range(i + 1, GROUP):
                cols[j] = cols[j] - cols[i] * tall(ratio[i, j])
                rows[j] = rows[j] - ratio[i, j] * rows[i]
            term = scaled * tall(rows[i])
            update = term if update is None else update + term
        work = work - update
    return work[:, step:width] * lax.rsqrt(pivots)[:, :step]


def invert(corner, out_ref, work_ref):
    size = corner.shape[0]
    step = STEP
    row = lax.broadcasted_iota(jnp.int32, (size, size), 0)
    col = lax.broadcasted_iota(jnp.int32, (size, size), 1)
    work_ref[:, :size] = corner
    work_ref[:, size:] = (row == col).astype(jnp.float32)
    small_row = lax.broadcasted_iota(jnp.int32, (step, step), 0)
    small_col = lax.broadcasted_iota(jnp.int32, (step, step), 1)
    eye = (small_row == small_col).astype(jnp.float32)
    for start in range(0, size, step):
        stop = start + step
        lead = eliminate(work_ref[start:stop, start:stop], eye, step)
        upper = matmul(lead, work_ref[start:stop, :])
        out_ref[start:stop, :] = upper[:, size:]
        if stop < size:
            work_ref[stop:, :] = work_ref[stop:, :] - matmul_tn(upper[:, stop:size], upper)


def inverse_kernel(lower_ref, out_ref, work_ref):
    side = lower_ref.shape[1]
    below = lower_ref[side : 2 * side, :]
    top = jnp.concatenate([lower_ref[:side, :], below.T], axis=1)
    bottom = jnp.concatenate([below, lower_ref[2 * side :, :]], axis=1)
    invert(jnp.concatenate([top, bottom], axis=0), out_ref, work_ref)


def lower_inverse(lower):
    size = 2 * lower.shape[1]
    return pl.pallas_call(
        inverse_kernel,
        out_shape=jax.ShapeDtypeStruct((size, size), jnp.float32),
        scratch_shapes=[pltpu.VMEM((size, 2 * size), jnp.float32)],
        name="lower_inverse",
    )(lower)


def parent_kernel(where_ref, inverse_ref, tops_ref, top_ref, parent_ref, out_ref):
    row_id, own_column = where_ref[0], where_ref[1]
    lead = PANEL // BLOCK
    blocks = tops_ref.shape[0]

    @pl.when(own_column >= lead)
    def _():
        upper = matmul(inverse_ref[...], top_ref[...])

        def body(block, carry):
            part = pl.ds(pl.multiple_of(block * BLOCK, BLOCK), BLOCK)
            factor = matmul(inverse_ref[...], tops_ref[block], HIGH)
            change = matmul_tn(factor, upper, HIGH)
            first = (row_id == 0) & (block < lead)
            out_ref[part, :] = parent_ref[part, :] - jnp.where(first, 0.0, change)
            return carry

        lax.fori_loop(0, blocks, body, 0)

    @pl.when(own_column < lead)
    def _():
        start = pl.multiple_of(jnp.minimum(own_column, lead - 1) * BLOCK, BLOCK)
        rows = inverse_ref[pl.ds(start, BLOCK), :]

        def body(block, carry):
            part = pl.ds(pl.multiple_of(block * BLOCK, BLOCK), BLOCK)
            out_ref[part, :] = matmul(rows, tops_ref[block]).T
            return carry

        lax.fori_loop(0, blocks, body, 0)


def parent_base(where, inverse, tops, top, parent):
    vmem = pl.BlockSpec(memory_space=pltpu.VMEM)
    return pl.pallas_call(
        parent_kernel,
        out_shape=jax.ShapeDtypeStruct(parent.shape, jnp.float32),
        in_specs=[pl.BlockSpec(memory_space=pltpu.SMEM), vmem, vmem, vmem, vmem],
        out_specs=vmem,
        name="parent_base",
    )(where, inverse, tops, top, parent)


def pick_kernel(index_ref, front_ref, out_ref):
    out_ref[0] = front_ref[...]


def pick_columns(index, front):
    rows = front.shape[0]
    count = index.shape[0]
    return pl.pallas_call(
        pick_kernel,
        out_shape=jax.ShapeDtypeStruct((count, rows, BLOCK), jnp.float32),
        grid_spec=pltpu.PrefetchScalarGridSpec(
            num_scalar_prefetch=1,
            grid=(count,),
            in_specs=[pl.BlockSpec((rows, BLOCK), lambda i, index: (0, index[i]))],
            out_specs=pl.BlockSpec((1, rows, BLOCK), lambda i, index: (i, 0, 0)),
        ),
        name="pick_columns",
    )(index, front)


def schur_kernel(
    slot_ref, live_ref, piece_ref, valid_ref, cols_ref, factor_ref, inverse_ref, block_ref,
    out_ref, tmp_ref, sems,
):
    leaves = live_ref.shape[0]
    bands = valid_ref.shape[0]

    def copy(leaf, dest):
        start = pl.multiple_of(piece_ref[dest] * BLOCK, BLOCK)
        piece = tmp_ref.at[leaf, pl.ds(start, BLOCK), :]
        item = leaf * bands + dest
        return pltpu.make_async_copy(piece, out_ref.at[item], sems.at[item])

    def each(leaf, act):
        for dest in range(bands):

            @pl.when(valid_ref[dest] > 0)
            def _(dest=dest):
                act(copy(leaf, dest))

    def start(leaf, carry):
        @pl.when(live_ref[leaf] > 0)
        def _():
            slot = slot_ref[leaf]
            block = matmul_nt(block_ref[slot], inverse_ref[...])
            tmp_ref[leaf] = cols_ref[slot] - matmul_nt(factor_ref[...], block)
            each(leaf, lambda copy: copy.start())

        return carry

    def finish(leaf, carry):
        @pl.when(live_ref[leaf] > 0)
        def _():
            each(leaf, lambda copy: copy.wait())

        return carry

    lax.fori_loop(0, leaves, start, 0)
    lax.fori_loop(0, leaves, finish, 0)


def schur_pieces(slot, live, piece, valid, cols, factor, inverse, blocks):
    leaves = slot.shape[0]
    bands = piece.shape[0]
    rows = factor.shape[0]
    smem = pl.BlockSpec(memory_space=pltpu.SMEM)
    vmem = pl.BlockSpec(memory_space=pltpu.VMEM)
    anywhere = pl.BlockSpec(memory_space=pl.ANY)
    return pl.pallas_call(
        schur_kernel,
        out_shape=jax.ShapeDtypeStruct((leaves * bands, BLOCK, BLOCK), jnp.float32),
        in_specs=[smem] * 4 + [vmem] * 4,
        out_specs=anywhere,
        scratch_shapes=[
            pltpu.VMEM((leaves, rows, BLOCK), jnp.float32),
            pltpu.SemaphoreType.DMA((leaves * bands,)),
        ],
        name="schur_pieces",
    )(slot, live, piece, valid, cols, factor, inverse, blocks)


def top_kernel(slot_ref, live_ref, row_ref, cols_ref, raw_ref, inverse_ref, block_ref, out_ref):
    @pl.when(row_ref[1] > 0)
    def _():
        part = pl.ds(pl.multiple_of(row_ref[0] * BLOCK, BLOCK), BLOCK)
        factor = matmul_nt(raw_ref[part, :], inverse_ref[...])

        def body(leaf, carry):
            @pl.when(live_ref[leaf] > 0)
            def _():
                slot = slot_ref[leaf]
                block = matmul_nt(block_ref[slot], inverse_ref[...])
                out_ref[leaf] = cols_ref[slot, part, :] - matmul_nt(factor, block)

            return carry

        lax.fori_loop(0, live_ref.shape[0], body, 0)


def top_pieces(slot, live, row, cols, raw, inverse, blocks):
    smem = pl.BlockSpec(memory_space=pltpu.SMEM)
    vmem = pl.BlockSpec(memory_space=pltpu.VMEM)
    return pl.pallas_call(
        top_kernel,
        out_shape=jax.ShapeDtypeStruct((slot.shape[0], BLOCK, BLOCK), jnp.float32),
        in_specs=[smem] * 3 + [vmem] * 4,
        out_specs=vmem,
        name="top_pieces",
    )(slot, live, row, cols, raw, inverse, blocks)


def place_kernel(slot_ref, base_ref, blocks_ref, out_ref, tmp_ref, sems):
    def copy(item):
        return pltpu.make_async_copy(blocks_ref.at[item], tmp_ref.at[item], sems.at[item])

    def start(item, carry):
        @pl.when(slot_ref[item] >= 0)
        def _():
            copy(item).start()

        return carry

    def finish(item, carry):
        slot = slot_ref[item]

        @pl.when(slot >= 0)
        def _():
            copy(item).wait()
            first = pl.multiple_of(slot * BLOCK, BLOCK)
            out_ref[pl.ds(first, BLOCK), :] += tmp_ref[item]

        return carry

    count = blocks_ref.shape[0]
    lax.fori_loop(0, count, start, 0)
    out_ref[...] = base_ref[...]
    lax.fori_loop(0, count, finish, 0)


def place_blocks(slots, base, blocks):
    vmem = pl.BlockSpec(memory_space=pltpu.VMEM)
    return pl.pallas_call(
        place_kernel,
        out_shape=jax.ShapeDtypeStruct(base.shape, jnp.float32),
        in_specs=[
            pl.BlockSpec(memory_space=pltpu.SMEM),
            vmem,
            pl.BlockSpec(memory_space=pl.ANY),
        ],
        out_specs=vmem,
        scratch_shapes=[
            pltpu.VMEM(blocks.shape, jnp.float32),
            pltpu.SemaphoreType.DMA((blocks.shape[0],)),
        ],
        name="place_blocks",
    )(slots, base, blocks)


def locate(values, usable, count):
    hit = (values[..., None, :] == jnp.arange(count)[:, None]) & usable[..., None, :]
    index = jnp.sum(jnp.where(hit, jnp.arange(values.shape[-1]), 0), axis=-1)
    return index.astype(jnp.int32), jnp.any(hit, axis=-1)


def at(value, index, axis=0):
    return lax.dynamic_index_in_dim(value, index, axis, keepdims=False)


def swapped_core(along):
    other = lax.ppermute(along, "col_1", [(0, 1), (1, 0)])
    first = lax.axis_index("col_1") == 0
    both = jnp.stack([jnp.where(first, along, other), jnp.where(first, other, along)], axis=1)
    return both.reshape(-1, *along.shape[1:])


def from_first(value, axis, stride=None):
    index = lax.axis_index(axis)
    stride = stride or lax.axis_size(axis) // 2
    while stride:
        value = tree_round(value, axis, index, stride)
        stride //= 2
    return value


def tree_round(value, axis, index, stride):
    pairs = [(i, i + stride) for i in range(0, lax.axis_size(axis), 2 * stride)]
    other = lax.ppermute(value, axis, pairs)
    return jnp.where(index % (2 * stride) == stride, other, value)


def eliminate_and_assemble(child_front, parent_front, block_map):
    front = child_front[0]
    parent = parent_front[:, 0, 0, :]
    grid_rows = lax.axis_size("row")
    grid_cols = lax.axis_size(COL)
    leaves = lax.axis_size("leaf")
    row_id = lax.axis_index("row")
    col_id = lax.axis_index(COL)
    leaf_id = lax.axis_index("leaf")
    rows = front.shape[0]
    child_blocks = rows // BLOCK
    lead = PANEL // BLOCK

    padded = jnp.concatenate([jnp.full((leaves, lead), -1, jnp.int32), block_map], axis=1)
    maps = padded.reshape(leaves, grid_rows, child_blocks)
    usable = maps >= 0
    band = maps // grid_cols
    residue = maps % grid_cols
    lo_index, lo_valid = locate(residue, usable, grid_cols)
    hi_index, hi_valid = locate(band, usable, grid_rows)
    own_lo_index, own_lo_valid = at(lo_index, leaf_id), at(lo_valid, leaf_id)
    column_index = at(own_lo_index, col_id, 1)
    column_valid = at(own_lo_valid, col_id, 1)

    half = grid_rows // 2
    deal = exchange(front[:, :PANEL].reshape(grid_cols, -1, PANEL), COL)[0]
    parent_top = tree_round(parent[:PANEL], "row", row_id, half)
    send_index = at(own_lo_index, col_id)
    deal, send_index, parent_top = lax.optimization_barrier((deal, send_index, parent_top))
    picked = pick_columns(send_index, front)
    along = spread(deal, "col_0", lax.axis_size("col_0"))
    parent_top = tree_round(parent_top, "row", row_id, half // 2)
    along, parent_top = lax.optimization_barrier((along, parent_top))
    raw = swapped_core(along)
    parent_top = from_first(parent_top, "row", half // 4)
    picked, raw, parent_top = lax.optimization_barrier((picked, raw, parent_top))
    cols = exchange(picked, COL)
    raw = raw.reshape(rows, PANEL)
    mine = lax.dynamic_slice_in_dim(raw, at(column_index, row_id) * BLOCK, BLOCK, 0)
    blocks = lax.all_gather(mine, "row")
    corner = jnp.concatenate([raw[:PANEL, :BLOCK], raw[BLOCK:PANEL, BLOCK:]])
    inverse = lower_inverse(from_first(corner, "row"))
    column_band = jnp.sum(
        jnp.where(jnp.arange(child_blocks) == column_index[:, None], at(band, leaf_id), 0), axis=-1
    )
    slot, slot_valid = locate(column_band, column_valid, leaves)
    live = slot_valid.astype(jnp.int32)
    piece = at(at(hi_index, leaf_id), row_id)
    valid = at(at(hi_valid, leaf_id), row_id)
    first = jnp.sum(
        jnp.where(jnp.arange(child_blocks) == piece[0], at(at(residue, leaf_id), row_id), 0)
    )
    row = jnp.stack([piece[0], (valid[0] & (first < lead)).astype(jnp.int32)])
    tops = top_pieces(slot, live, row, cols, raw, inverse, blocks)
    factor = matmul_nt(raw, inverse)
    pieces = schur_pieces(slot, live, piece, valid.astype(jnp.int32), cols, factor, inverse, blocks)

    own_column = leaf_id * grid_cols + col_id
    present = jnp.any((maps == own_column) & usable, axis=(1, 2))
    row_slot = jnp.sum(
        jnp.where(jnp.arange(child_blocks) == hi_index[..., None], residue[:, :, None, :], 0),
        axis=-1,
    )
    row_slot = jnp.where(hi_valid & present[:, None, None], row_slot, -1).astype(jnp.int32)

    tops = exchange(tops.reshape(leaves * grid_rows, -1, BLOCK), LEAF_ROW)
    chosen = row_slot[:, :, 0].reshape(-1) == jnp.arange(lead)[:, None]
    top = jnp.sum(jnp.where(chosen[:, :, None, None], tops, 0.0), axis=1)
    top = spread(top, "row", grid_rows).transpose(1, 0, 2, 3).reshape(PANEL, BLOCK) + parent_top
    arrived = exchange(pieces, LEAF_ROW)

    every_leaf = lax.all_gather(top, "leaf")
    tops = lax.all_gather(at(every_leaf, row_id), COL)
    corner = from_first(every_leaf[0], "col_0")
    corner = swapped_core(corner[None])
    corner = lower_inverse(jnp.concatenate([corner[0], corner[1, BLOCK:]]))
    place = jnp.stack([row_id, own_column]).astype(jnp.int32)
    base = parent_base(place, corner, tops, top, parent)
    slots = jnp.where(own_column < lead, -1, at(row_slot, row_id, 2)).reshape(-1)
    result = place_blocks(slots, base, arrived)
    return (factor[None], result[:, None, None, :])


def solution(mesh):
    torus = Mesh(
        mesh.devices.reshape(mesh.shape["leaf"], mesh.shape["row"], 4, 2),
        ("leaf", "row", "col_0", "col_1"),
    )
    in_specs = (P("leaf", "row", COL), P("row", None, LEAF_COL, None), P())
    out_specs = (P("leaf", "row", None), P("row", None, LEAF_COL, None))
    return jax.shard_map(
        eliminate_and_assemble, mesh=torus, in_specs=in_specs, out_specs=out_specs, check_vma=False
    )
```
